32 devices in a mesh: dp: 4 (over z), expert: 8 (over y, x, core).
Axes of the slice: x: 2, y: 2, z: 4, core: 2. Of those that a mesh axis runs over, the one named last changes fastest.
Arguments:
- grad_parts: bfloat16 [4, 32, 128, 2048], P('dp', 'expert'), may hold values from -6 to 6
- first_moment: float32 [32, 128, 2048], P('expert', None, 'dp'), may hold values from -4 to 4
- second_moment: float32 [32, 128, 2048], P('expert', None, 'dp'), may hold values from 0.05 to 2
- master_weight: float32 [32, 128, 2048], P('expert', None, 'dp'), may hold values from -6 to 6
- old_owner: int32 [28], replicated, may hold values from 0 to 6, as said below
- new_owner: int32 [28], replicated, may hold values from 0 to 7, as said below
Outputs:
- new_master: float32 [48, 128, 2048], P('expert', None, 'dp')
- new_first: float32 [48, 128, 2048], P('expert', None, 'dp')
- new_second: float32 [48, 128, 2048], P('expert', None, 'dp')
- new_params: bfloat16 [48, 128, 2048], P('expert')
The draws below stay inside these ranges and needn't reach their ends.
Inputs may be any that keep to these rules, and one draw needn't show every extreme that they name: `old_owner`: tiles are owned by devices 0 to 6 of the expert axis, exactly 4 each; the other devices own none, and their slots of the old-layout arrays are never read. `new_owner`: each device owns at most 6 tiles and some own exactly 6; the tiles of one old owner go to different new owners.
All inputs are finite; a program needn't handle non-finite values.
Results may differ from the reference program's by a relative error of at most 0.0085.
Values may be sent and summed in bfloat16 or wider, within the bound.
A program may use at most 128 MiB of HBM per device.

```python
import math
import jax
import jax.numpy as jnp
from jax import lax

FF = 2048
TILE_ROWS = 128
OLD_SLOTS = 4
OLD_DEV = 7
NEW_SLOTS = 6
HOT = 1
TILES = 28
N_DP = 4
N_EXPERT = 8


def owner_maps(key):
    key_perm, key_place = jax.random.split(jax.random.fold_in(key, 7))
    shuffle = jax.random.permutation(key_perm, TILES).astype(jnp.int32)
    counter = jnp.arange(TILES, dtype=jnp.int32)
    old_map = jnp.zeros((TILES,), jnp.int32).at[shuffle].set(counter // OLD_SLOTS)
    device_ids = jnp.arange(N_EXPERT, dtype=jnp.int32)
    remaining = TILES - HOT * NEW_SLOTS
    base_load = remaining // (N_EXPERT - HOT)
    extra_load = remaining % (N_EXPERT - HOT)
    load_sizes = jnp.where(device_ids < HOT, NEW_SLOTS, base_load + (device_ids - HOT < extra_load).astype(jnp.int32))
    bounds = jnp.cumsum(load_sizes).astype(jnp.int32)
    position = jnp.sum((counter[:, None] >= bounds[None, :]).astype(jnp.int32), axis=1)
    slot_part = counter // OLD_DEV
    owner_part = counter % OLD_DEV
    tile_ids = shuffle[owner_part * OLD_SLOTS + slot_part]
    relabel = jax.random.permutation(key_place, N_EXPERT).astype(jnp.int32)
    new_map = jnp.zeros((TILES,), jnp.int32).at[tile_ids].set(relabel[position])
    return (old_map, new_map)


def draw_old_owner(key, part):
    return owner_maps(key)[0]


def draw_new_owner(key, part):
    return owner_maps(key)[1]


def block_scale(own_key, dims, shards, least, high):
    gain = 1.0
    for axis_at, shards_of in shards:
        draws = jax.random.uniform(jax.random.fold_in(jax.random.fold_in(own_key, 6), axis_at), (shards_of,), jnp.float32, least / len(shards), high / len(shards))
        gain = gain * jnp.repeat(jnp.exp(draws), dims[axis_at] // shards_of).reshape((-1,) + (1,) * (len(dims) - 1 - axis_at))
    return gain


def noise(key, dims, width, reach, cuts=(), kind=jnp.bfloat16):
    array = jax.random.normal(key, dims, jnp.float32) * width
    if len(cuts) > 0:
        array = block_scale(key, dims, cuts, -0.22, 0.18) * array
    return jnp.clip(array, min=-reach, max=reach).astype(kind)


def setup_inputs(seed: int = 0) -> dict:
    keys = jax.random.split(jax.random.key(seed), 7)
    return {
        "grad_parts": noise(keys[0], (N_DP, N_EXPERT * OLD_SLOTS, TILE_ROWS, FF), 1.0, 6.0, ((0, 4), (1, 8))),
        "first_moment": noise(keys[1], (N_EXPERT * OLD_SLOTS, TILE_ROWS, FF), 0.3, 4.0, ((0, 8), (2, 4)), jnp.float32),
        "second_moment": jnp.clip(jnp.exp(math.log(2.0) - 3.6888794 * jax.random.uniform(keys[2], (N_EXPERT * OLD_SLOTS, TILE_ROWS, FF), jnp.float32) ** block_scale(keys[2], (N_EXPERT * OLD_SLOTS, TILE_ROWS, FF), ((0, 8), (2, 4)), -0.2, 0.2)), 0.05, 2.0),
        "master_weight": noise(keys[3], (N_EXPERT * OLD_SLOTS, TILE_ROWS, FF), 0.5, 6.0, ((0, 8), (2, 4)), jnp.float32),
        "old_owner": draw_old_owner(jax.random.fold_in(keys[6], 71), 0),
        "new_owner": draw_new_owner(jax.random.fold_in(keys[6], 71), 0),
    }


def slot_ranks(owner, count):
    matches = (owner[:, None] == jnp.arange(count, dtype=jnp.int32)[None, :]).astype(jnp.int32)
    before = jnp.cumsum(matches, axis=0) - matches
    return lax.optimization_barrier(jnp.sum(before * matches, axis=1)).astype(jnp.int32)

def adam_step(gradient, moment_one, moment_two, weight):
    moment_one = 0.9 * moment_one + 0.1 * gradient
    moment_two = 0.95 * moment_two + 0.05 * gradient * gradient
    update = moment_one / (1.0 - 0.9 ** 50) / (jnp.sqrt(moment_two / (1.0 - 0.95 ** 50)) + 1e-08)
    weight = weight - 0.05 * (update + 0.1 * weight)
    return (weight, moment_one, moment_two)

def reference(grad_parts, first_moment, second_moment, master_weight, old_owner, new_owner):
    old_rank = slot_ranks(old_owner, N_EXPERT)
    new_rank = slot_ranks(new_owner, N_EXPERT)
    source_rows = (old_owner * OLD_SLOTS + old_rank).astype(jnp.int32)
    target_rows = (new_owner * NEW_SLOTS + new_rank).astype(jnp.int32)
    gradient = jnp.zeros((TILES, TILE_ROWS, FF), jnp.float32)
    for replica in range(N_DP):
        gradient = gradient + grad_parts[replica][source_rows].astype(jnp.float32)
    weight, moment_one, moment_two = adam_step(gradient, first_moment[source_rows], second_moment[source_rows], master_weight[source_rows])
    empty = jnp.zeros((N_EXPERT * NEW_SLOTS, TILE_ROWS, FF), jnp.float32)
    new_master = empty.at[target_rows].set(weight)
    new_first = empty.at[target_rows].set(moment_one)
    new_second = empty.at[target_rows].set(moment_two)
    return (new_master, new_first, new_second, new_master.astype(jnp.bfloat16))
```

```python
import functools

import jax
import jax.numpy as jnp
from jax import lax
from jax.experimental import pallas as pl
from jax.experimental.pallas import tpu as pltpu
from jax.sharding import PartitionSpec as P

MESH = pl.DeviceIdType.MESH
ROWS = 16
AHEAD = 1
HOP = 1
MAIL = 2
WIDE = 2
PLAN = (1, 0)


def early(c):
    return PLAN[c % len(PLAN)] == 1


def adam_step(gradient, moment_one, moment_two, weight):
    moment_one = 0.9 * moment_one + 0.1 * gradient
    moment_two = 0.95 * moment_two + 0.05 * gradient * gradient
    update = moment_one / (1.0 - 0.9**50) / (jnp.sqrt(moment_two / (1.0 - 0.95**50)) + 1e-08)
    weight = weight - 0.05 * (update + 0.1 * weight)
    return (weight, moment_one, moment_two)


def kernel(dp, peers, owners, chunks, old_ref, new_ref, g_hbm, m_hbm, v_hbm, w_hbm, *rest):
    moments, params, rest = rest[0], rest[1], rest[2:]
    g, state, part, up, down, stay = rest[:6]
    rest = rest[6:]
    fresh, mail, inbox, wide, wide_mail, wide_inbox = (rest[i * chunks : (i + 1) * chunks] for i in range(6))
    (in_sem, up_send, up_recv, down_send, down_recv, x_send, x_recv, w_send, w_recv,
     gu_send, gu_recv, gd_send, gd_recv) = rest[6 * chunks :]
    z = lax.axis_index("dp")
    e = lax.axis_index("expert")
    cols = stay.shape[-1]
    new_slots = params.shape[0]
    mine = pl.ds(pl.multiple_of(z * cols, cols), cols)
    owns = e < owners

    loads = [pltpu.make_async_copy(g_hbm.at[0], g, in_sem.at[0])]
    loads += [
        pltpu.make_async_copy(ref, state.at[i], in_sem.at[i + 1])
        for i, ref in enumerate((m_hbm, v_hbm, w_hbm))
    ]
    for load in loads:
        load.start()

    barrier = pltpu.get_barrier_semaphore()
    for step in range(1, peers):
        pl.semaphore_signal(
            barrier, inc=1, device_id={"expert": lax.rem(e + step, peers)}, device_id_type=MESH
        )

    @pl.when(z > 0)
    def _():
        pl.semaphore_signal(barrier, inc=1, device_id={"dp": z - 1}, device_id_type=MESH)

    @pl.when(z < dp - 1)
    def _():
        pl.semaphore_signal(barrier, inc=1, device_id={"dp": z + 1}, device_id_type=MESH)

    inner = (z > 0).astype(jnp.int32) + (z < dp - 1).astype(jnp.int32)
    pl.semaphore_wait(barrier, peers - 1 + inner)
    for load in loads:
        load.wait()

    tiles = old_ref.shape[0]
    targets = [lax.rem(e + step, peers) for step in range(peers)]

    def route(tile, carry):
        sent, taken, slots, sources = carry
        old, new = old_ref[tile], new_ref[tile]
        leaves, comes = old == e, new == e
        slots = tuple(jnp.where(leaves & (new == to), sent, slot) for to, slot in zip(targets, slots))
        sources = tuple(
            jnp.where(comes & (taken == slot), old, source) for slot, source in enumerate(sources)
        )
        return sent + leaves.astype(jnp.int32), taken + comes.astype(jnp.int32), slots, sources

    def rows(c):
        return pl.ds(c * ROWS, ROWS)

    def block(k):
        return pl.ds(k * cols, cols)

    def up_copy(c, k, raw):
        src = g.at[:, rows(c), block(k)] if raw else part.at[k, :, rows(c)]
        return pltpu.make_async_remote_copy(
            src, up.at[k, :, rows(c)], up_send.at[c, k], up_recv.at[c, k],
            device_id={"dp": z + 1}, device_id_type=MESH,
        )

    def down_copy(c, k, raw):
        src = g.at[:, rows(c), block(k)] if raw else part.at[k, :, rows(c)]
        return pltpu.make_async_remote_copy(
            src, down.at[k, :, rows(c)], down_send.at[c, k], down_recv.at[c, k],
            device_id={"dp": z - 1}, device_id_type=MESH,
        )

    def gather_copy(c, k, going_up):
        send, recv = (gu_send, gu_recv) if going_up else (gd_send, gd_recv)
        where = wide[c].at[:, :, block(k)] if early(c) else params.at[:, rows(c), block(k)]
        return pltpu.make_async_remote_copy(
            where, where, send.at[c, k], recv.at[c, k],
            device_id={"dp": z + 1 if going_up else z - 1}, device_id_type=MESH,
        )

    def mail_copy(c, to, source):
        return pltpu.make_async_remote_copy(
            mail[c].at[to], inbox[c].at[source], x_send.at[c, to], x_recv.at[c, source],
            device_id={"expert": to}, device_id_type=MESH,
        )

    def wide_copy(c, to, source):
        return pltpu.make_async_remote_copy(
            wide_mail[c].at[to], wide_inbox[c].at[source], w_send.at[c, to], w_recv.at[c, source],
            device_id={"expert": to}, device_id_type=MESH,
        )

    def first_sends(c):
        @pl.when(owns & (z == 0))
        def _():
            for k in range(dp - 1, 0, -1):
                up_copy(c, k, True).start()

        @pl.when(owns & (z == dp - 1))
        def _():
            for k in range(dp - 1):
                down_copy(c, k, True).start()

    def relay_up(c, at):
        for k in range(dp - 1, at, -1):
            up_copy(c, k, False).wait_recv()
            total = g[:, rows(c), block(k)].astype(jnp.float32) + up[k, :, rows(c)].astype(jnp.float32)
            part[k, :, rows(c)] = total.astype(jnp.bfloat16)
            up_copy(c, k, False).start()

    def relay_down(c, at):
        for k in range(at):
            down_copy(c, k, False).wait_recv()
            total = g[:, rows(c), block(k)].astype(jnp.float32) + down[k, :, rows(c)].astype(jnp.float32)
            part[k, :, rows(c)] = total.astype(jnp.bfloat16)
            down_copy(c, k, False).start()

    def relay(c, at, going_up):
        @pl.when(owns & (z == at))
        def _():
            (relay_up if going_up else relay_down)(c, at)

    def update(c):
        @pl.when(owns)
        def _():
            stay[...] = g[:, rows(c), mine].astype(jnp.float32)
            for k in range(dp):
                @pl.when(z == k)
                def _():
                    if k > 0:
                        up_copy(c, k, False).wait_recv()
                        stay[...] += up[k, :, rows(c)].astype(jnp.float32)
                    if k < dp - 1:
                        down_copy(c, k, False).wait_recv()
                        stay[...] += down[k, :, rows(c)].astype(jnp.float32)
            for slot in range(stay.shape[0]):
                values = adam_step(
                    stay[slot], state[0, slot, rows(c)], state[1, slot, rows(c)], state[2, slot, rows(c)]
                )
                values = [value.astype(jnp.bfloat16) for value in values]
                if early(c):
                    wide[c][slot, :, mine] = values.pop(0)
                for i, value in enumerate(values):
                    fresh[c][slot, i] = value
            if early(c):
                gather(c)
            for to, slot in zip(targets[1:], slots[1:]):
                mail[c][to] = fresh[c][slot]
                mail_copy(c, to, e).start()
            inbox[c][e] = fresh[c][slots[0]]

    def gather(c):
        for k in range(dp):
            @pl.when(z == k)
            def _():
                if k < dp - 1:
                    gather_copy(c, k, True).start()
                if k > 0:
                    gather_copy(c, k, False).start()

    def forward(c, hop):
        for at in range(1, dp - 1):
            @pl.when((owns & (z == at)) if early(c) else (z == at))
            def _():
                for k, going_up in ((at - hop, True), (at + hop, False)):
                    if 0 <= k < dp:
                        gather_copy(c, k, going_up).wait_recv()
                        gather_copy(c, k, going_up).start()

    def gathered(c):
        @pl.when(z == dp - 1)
        def _():
            for k in range(dp - 1):
                gather_copy(c, k, True).wait_recv()

        @pl.when(z == 0)
        def _():
            for k in range(1, dp):
                gather_copy(c, k, False).wait_recv()

    def post_wide(c):
        @pl.when(owns)
        def _():
            gathered(c)
            for to, slot in zip(targets[1:], slots[1:]):
                wide_mail[c][to] = wide[c][slot]
                wide_copy(c, to, e).start()
            wide_inbox[c][e] = wide[c][slots[0]]

    def deliver(c):
        for source in range(owners):
            @pl.when(e != source)
            def _():
                mail_copy(c, source, source).wait_recv()
                if early(c):
                    wide_copy(c, source, source).wait_recv()

        for slot in range(new_slots):
            present = taken > slot

            def kept(value):
                return jnp.where(present, value, jnp.zeros_like(value))

            if early(c):
                params[slot, rows(c)] = kept(wide_inbox[c][sources[slot]])
            else:
                params[slot, rows(c), mine] = kept(inbox[c][sources[slot], 0])
            first = 0 if early(c) else 1
            for i in range(2):
                moments[i, slot, rows(c)] = kept(inbox[c][sources[slot], first + i])
        if not early(c):
            gather(c)

    for c in range(min(AHEAD, chunks)):
        first_sends(c)
    zero = jnp.int32(0)
    _, taken, slots, sources = lax.fori_loop(
        0, tiles, route, (zero, zero, (zero,) * peers, (zero,) * new_slots)
    )
    slots = tuple(jnp.minimum(slot, stay.shape[0] - 1) for slot in slots)
    sources = tuple(jnp.minimum(source, owners - 1) for source in sources)
    jobs = []
    for c in range(chunks):
        if c >= AHEAD:
            jobs.append((c - AHEAD + 1, c, first_sends, (c,)))
        for at in range(1, dp - 1):
            jobs.append((c + at * HOP, c, relay, (c, at, True)))
            jobs.append((c + (dp - 1 - at) * HOP, c, relay, (c, at, False)))
        now = c + (dp - 1) * HOP
        jobs.append((now, c, update, (c,)))
        if not early(c):
            now += MAIL
            jobs.append((now, c, deliver, (c,)))
        for hop in range(1, dp - 1):
            jobs.append((now + hop * HOP, c, forward, (c, hop)))
        now += (dp - 1) * HOP
        if early(c):
            jobs.append((now, c, post_wide, (c,)))
            jobs.append((now + WIDE, c, deliver, (c,)))
        else:
            jobs.append((now, c, gathered, (c,)))
    for _, _, job, args in sorted(jobs, key=lambda item: item[:2]):
        job(*args)

    for c in range(chunks):
        for k in range(dp):
            reach = owns if early(c) else True

            @pl.when(reach & (z >= k) & (z < dp - 1))
            def _():
                gather_copy(c, k, True).wait_send()

            @pl.when(reach & (z <= k) & (z > 0))
            def _():
                gather_copy(c, k, False).wait_send()

        @pl.when(owns)
        def _():
            for k in range(1, dp):
                @pl.when(z < k)
                def _():
                    up_copy(c, k, False).wait_send()
            for k in range(dp - 1):
                @pl.when(z > k)
                def _():
                    down_copy(c, k, False).wait_send()
            for to in targets[1:]:
                mail_copy(c, to, e).wait_send()
                if early(c):
                    wide_copy(c, to, e).wait_send()


def widen(moments, params, w_out, m_out, v_out, p_out, staged, sems, sem):
    new_slots, _, cols = w_out.shape
    z = lax.axis_index("dp")
    mine = pl.ds(pl.multiple_of(z * cols, cols), cols)
    copies = [pltpu.make_async_copy(params, p_out, sem)]
    copies[0].start()
    for slot in range(new_slots):
        parts = (params.at[slot, :, mine], moments.at[0, slot], moments.at[1, slot])
        for i, (part, out) in enumerate(zip(parts, (w_out, m_out, v_out))):
            staged[i, slot] = part[...].astype(jnp.float32)
            copies.append(pltpu.make_async_copy(staged.at[i, slot], out.at[slot], sems.at[i, slot]))
            copies[-1].start()
    for copy in copies:
        copy.wait()


def shards(grad_parts, first_moment, second_moment, master_weight, old_owner, new_owner):
    dp = lax.axis_size("dp")
    peers = lax.axis_size("expert")
    old_slots, tile_rows, cols = first_moment.shape
    owners = old_owner.shape[0] // old_slots
    new_slots = min(old_slots + old_slots // 2, peers - peers // 5)
    chunks = tile_rows // ROWS
    bf16, f32 = jnp.bfloat16, jnp.float32
    dma = pltpu.SemaphoreType.DMA
    any_space = pl.BlockSpec(memory_space=pl.ANY)
    smem = pl.BlockSpec(memory_space=pltpu.SMEM)
    master = jax.ShapeDtypeStruct((new_slots, tile_rows, cols), f32)
    scratch = [
        pltpu.VMEM((old_slots, tile_rows, dp * cols), bf16),
        pltpu.VMEM((3, old_slots, tile_rows, cols), f32),
        pltpu.VMEM((dp, old_slots, tile_rows, cols), bf16),
        pltpu.VMEM((dp, old_slots, tile_rows, cols), bf16),
        pltpu.VMEM((dp, old_slots, tile_rows, cols), bf16),
        pltpu.VMEM((old_slots, ROWS, cols), f32),
    ]
    first = [early(c) for c in range(chunks)]
    kept = [2 if flag else 3 for flag in first]
    width = [dp * cols if flag else 128 for flag in first]
    span = [ROWS if flag else 16 for flag in first]
    scratch += [pltpu.VMEM((old_slots, n, ROWS, cols), bf16) for n in kept]
    scratch += [pltpu.VMEM((peers, n, ROWS, cols), bf16) for n in kept]
    scratch += [pltpu.VMEM((owners, n, ROWS, cols), bf16) for n in kept]
    scratch += [pltpu.VMEM((old_slots, r, n), bf16) for r, n in zip(span, width)]
    scratch += [pltpu.VMEM((peers, r, n), bf16) for r, n in zip(span, width)]
    scratch += [pltpu.VMEM((owners, r, n), bf16) for r, n in zip(span, width)]
    scratch += [dma((4,))] + [dma((chunks, dp))] * 4 + [dma((chunks, peers))] * 4
    scratch += [dma((chunks, dp))] * 4
    results = new_slots * tile_rows * cols * (4 + 2 * dp)
    vmem = pl.BlockSpec(memory_space=pltpu.VMEM)
    moments, params = pl.pallas_call(
        functools.partial(kernel, dp, peers, owners, chunks),
        out_shape=(
            pltpu.VMEM((2, new_slots, tile_rows, cols), bf16),
            pltpu.VMEM((new_slots, tile_rows, dp * cols), bf16),
        ),
        in_specs=[smem] * 2 + [any_space] * 4,
        out_specs=(vmem,) * 2,
        scratch_shapes=scratch,
        compiler_params=pltpu.CompilerParams(
            collective_id=0, has_side_effects=True, vmem_limit_bytes=67043328 - results - 2**19
        ),
    )(old_owner, new_owner, grad_parts, first_moment, second_moment, master_weight)
    return pl.pallas_call(
        widen,
        out_shape=(master,) * 3
        + (jax.ShapeDtypeStruct((new_slots, tile_rows, dp * cols), bf16),),
        in_specs=[vmem] * 2,
        out_specs=(any_space,) * 4,
        scratch_shapes=[pltpu.VMEM((3, new_slots, tile_rows, cols), f32), dma((3, new_slots)), dma],
        compiler_params=pltpu.CompilerParams(vmem_limit_bytes=2**24),
    )(moments, params)


def solution(mesh):
    placed = (
        P("dp", "expert", None, None),
        P("expert", None, "dp"),
        P("expert", None, "dp"),
        P("expert", None, "dp"),
        P(),
        P(),
    )
    return jax.shard_map(
        shards,
        mesh=mesh,
        in_specs=placed,
        out_specs=(
            P("expert", None, "dp"),
            P("expert", None, "dp"),
            P("expert", None, "dp"),
            P("expert", None, None),
        ),
        check_vma=False,
    )
```

```python
import functools

import jax
import jax.numpy as jnp
from jax import lax
from jax.experimental import pallas as pl
from jax.experimental.pallas import tpu as pltpu
from jax.sharding import PartitionSpec as P

MESH = pl.DeviceIdType.MESH
ROWS = 16
PLAN = (1, 1, 0, 1, 0, 1, 0, 0)
TABLE = ((('U', 0, 3), ('U', 1, 3), ('U', 2, 3), ('U', 2, 2), ('U', 0, 2), ('U', 3, 3), ('U', 4, 3), ('U', 2, 1), ('U', 0, 1), ('U', 1, 2), ('U', 4, 2), ('X', 0, 0), ('M', 0, 0), ('X', 1, 0), ('M', 1, 0), ('X', 2, 0), ('M', 2, 0), ('U', 1, 1), ('U', 5, 3), ('U', 6, 3), ('X', 3, 0), ('M', 3, 0), ('U', 4, 1), ('X', 4, 0), ('M', 4, 0), ('U', 3, 2), ('U', 6, 2), ('V', 2, 0), ('U', 7, 3), ('W', 0, 0), ('U', 3, 1), ('U', 7, 2), ('U', 6, 1), ('V', 4, 0), ('W', 1, 0), ('X', 5, 0), ('X', 6, 0), ('U', 5, 2), ('V', 0, 0), ('M', 6, 0), ('U', 7, 1), ('U', 5, 1), ('M', 5, 0), ('V', 1, 0), ('Z', 2, 0), ('X', 7, 0), ('M', 7, 0), ('V', 6, 0), ('W', 3, 0), ('Z', 4, 0), ('V', 7, 0), ('W', 5, 0), ('V', 3, 0), ('Z', 6, 0), ('V', 5, 0), ('Z', 7, 0)), (('U', 0, 3), ('U', 1, 3), ('U', 2, 3), ('D', 0, 0), ('U', 2, 2), ('D', 1, 0), ('U', 0, 2), ('D', 2, 0), ('U', 3, 3), ('U', 4, 3), ('X', 2, 0), ('M', 2, 0), ('D', 3, 0), ('X', 0, 0), ('M', 0, 0), ('D', 4, 0), ('U', 1, 2), ('U', 4, 2), ('F', 0, 0), ('F', 0, 2), ('V', 2, 0), ('F', 1, 0), ('X', 1, 0), ('M', 1, 0), ('U', 5, 3), ('F', 0, 3), ('W', 0, 0), ('U', 6, 3), ('F', 2, 2), ('F', 3, 0), ('F', 1, 3), ('X', 4, 0), ('M', 4, 0), ('F', 1, 2), ('U', 3, 2), ('D', 5, 0), ('U', 6, 2), ('D', 6, 0), ('W', 1, 0), ('F', 2, 0), ('F', 3, 3), ('V', 0, 0), ('U', 7, 3), ('X', 3, 0), ('U', 7, 2), ('V', 4, 0), ('M', 3, 0), ('F', 2, 3), ('X', 6, 0), ('D', 7, 0), ('F', 4, 0), ('M', 6, 0), ('F', 3, 2), ('F', 5, 0), ('V', 1, 0), ('U', 5, 2), ('F', 4, 2), ('X', 7, 0), ('M', 7, 0), ('F', 4, 3), ('F', 5, 3), ('X', 5, 0), ('W', 3, 0), ('V', 6, 0), ('F', 6, 0), ('F', 5, 2), ('V', 7, 0), ('W', 5, 0), ('F', 6, 2), ('F', 6, 3), ('F', 7, 0), ('F', 7, 2), ('V', 3, 0), ('M', 5, 0), ('F', 7, 3), ('V', 5, 0)))


def EARLY(c):
    return PLAN[c] == 1


def ORDERS(dp, chunks, role):
    return TABLE[role]


def adam_step(gradient, moment_one, moment_two, weight):
    moment_one = 0.9 * moment_one + 0.1 * gradient
    moment_two = 0.95 * moment_two + 0.05 * gradient * gradient
    update = moment_one / (1.0 - 0.9**50) / (jnp.sqrt(moment_two / (1.0 - 0.95**50)) + 1e-08)
    weight = weight - 0.05 * (update + 0.1 * weight)
    return (weight, moment_one, moment_two)


def job_list(dp, chunks, role):
    jobs = []
    for c in range(chunks):
        jobs += [("U", c, k) for k in range(dp - 1, role, -1)] + [("D", c, k) for k in range(role)]
        jobs += [("X", c, 0), ("M", c, 0)]
        jobs += [("F", c, k) for k in range(role - 1, -1, -1)]
        if role > 0:
            jobs += [("F", c, k) for k in range(role + 1, dp)]
        if EARLY(c):
            jobs.append(("W", c, 0))
        jobs.append(("V", c, 0))
        if role == 0 and not EARLY(c):
            jobs.append(("Z", c, 0))
    return jobs


def kernel(dp, peers, owners, chunks, old_ref, new_ref, g_hbm, m_hbm, v_hbm, w_hbm, *rest):
    moments, params, rest = rest[0], rest[1], rest[2:]
    g, state, part, line = rest[:4]
    rest = rest[4:]
    fresh, mail, inbox, wide, wide_mail, wide_inbox = (rest[i * chunks : (i + 1) * chunks] for i in range(6))
    (g_sem, in_sem, s_send, s_recv, a_send, a_recv, x_send, x_recv, w_send, w_recv) = rest[6 * chunks :]
    z = lax.axis_index("dp")
    e = lax.axis_index("expert")
    old_slots, cols = state.shape[1], state.shape[-1]
    new_slots = params.shape[0]
    far = jnp.where(z < dp // 2, 0, 1)
    place = jnp.where(z < dp // 2, z, dp - 1 - z)
    ahead = 1 - 2 * far
    mine = pl.ds(pl.multiple_of(z * cols, cols), cols)
    owns = e < owners

    if peers & (peers - 1):
        targets = [lax.rem(e + step, peers) for step in range(peers)]
    else:
        bits = [1 << i for i in range(peers.bit_length() - 1)]
        turns = {bit: bit * (1 - 2 * lax.rem(e // bit, 2)) for bit in bits}
        targets = [e + sum(turns[bit] for bit in bits if mask & bit) for mask in (0, *range(peers - 1, 0, -1))]

    def rows(c):
        return pl.ds(c * ROWS, ROWS)

    def real(k):
        return k + far * (dp - 1 - 2 * k)

    def block(k):
        return pl.ds(pl.multiple_of(real(k) * cols, cols), cols)

    def way(right):
        return far if right else 1 - far

    def beside(right):
        return {"dp": z + ahead if right else z - ahead}

    barrier = pltpu.get_barrier_semaphore()
    for to in targets[1:]:
        pl.semaphore_signal(barrier, inc=1, device_id={"expert": to}, device_id_type=MESH)
    for step in (-1, 1):
        @pl.when((z + step >= 0) & (z + step < dp))
        def _():
            pl.semaphore_signal(barrier, inc=1, device_id={"dp": z + step}, device_id_type=MESH)

    g_loads = [
        pltpu.make_async_copy(g_hbm.at[0, :, rows(c)], g.at[:, rows(c)], g_sem.at[c]) for c in range(chunks)
    ]
    loads = [
        pltpu.make_async_copy(ref, state.at[i], in_sem.at[i]) for i, ref in enumerate((m_hbm, v_hbm, w_hbm))
    ]

    @pl.when(owns)
    def _():
        for load in g_loads[:1] + loads + g_loads[1:]:
            load.start()

    inner = (z > 0).astype(jnp.int32) + (z < dp - 1).astype(jnp.int32)
    pl.semaphore_wait(barrier, peers - 1 + inner)

    def route(tile, carry):
        sent, taken, slots, sources = carry
        old, new = old_ref[tile], new_ref[tile]
        leaves, comes = old == e, new == e
        slots = tuple(jnp.where(leaves & (new == to), sent, slot) for to, slot in zip(targets, slots))
        sources = tuple(
            jnp.where(comes & (taken == slot), old, source) for slot, source in enumerate(sources)
        )
        return sent + leaves.astype(jnp.int32), taken + comes.astype(jnp.int32), slots, sources

    def sum_copy(c, k, right, raw=False):
        src = g.at[:, rows(c), block(k)] if raw else part.at[real(k), :, rows(c)]
        at = (way(right), c, real(k))
        return pltpu.make_async_remote_copy(
            src, line.at[way(right), real(k), :, rows(c)], s_send.at[at], s_recv.at[at],
            device_id=beside(right), device_id_type=MESH,
        )

    def gather_copy(c, k, right):
        where = wide[c].at[:, :, block(k)] if EARLY(c) else params.at[:, rows(c), block(k)]
        at = (way(right), c, real(k))
        return pltpu.make_async_remote_copy(
            where, where, a_send.at[at], a_recv.at[at], device_id=beside(right), device_id_type=MESH,
        )

    def mail_copy(c, to, source):
        return pltpu.make_async_remote_copy(
            mail[c].at[to], inbox[c].at[source], x_send.at[c, to], x_recv.at[c, source],
            device_id={"expert": to}, device_id_type=MESH,
        )

    def wide_copy(c, to, source):
        return pltpu.make_async_remote_copy(
            wide_mail[c].at[to], wide_inbox[c].at[source], w_send.at[c, to], w_recv.at[c, source],
            device_id={"expert": to}, device_id_type=MESH,
        )

    def arrived(c, k, right):
        return line[way(right), real(k), :, rows(c)].astype(jnp.float32)

    def add_and_send(c, k, right):
        sum_copy(c, k, right).wait_recv()
        total = g[:, rows(c), block(k)].astype(jnp.float32) + arrived(c, k, right)
        part[real(k), :, rows(c)] = total.astype(jnp.bfloat16)
        sum_copy(c, k, right).start()

    def gather(c, role):
        gather_copy(c, role, True).start()
        if role > 0:
            gather_copy(c, role, False).start()

    def update(c, role):
        sides = [right for right in (True, False) if role > 0 or not right]
        for right in sides:
            sum_copy(c, role, right).wait_recv()
        for slot in range(old_slots):
            gradient = g[slot, rows(c), mine].astype(jnp.float32)
            for right in sides:
                gradient += line[way(right), z, slot, rows(c)].astype(jnp.float32)
            values = adam_step(
                gradient, state[0, slot, rows(c)], state[1, slot, rows(c)], state[2, slot, rows(c)]
            )
            values = [value.astype(jnp.bfloat16) for value in values]
            if EARLY(c):
                wide[c][slot, :, mine] = values.pop(0)
            for i, value in enumerate(values):
                fresh[c][slot, i] = value
        if EARLY(c):
            gather(c, role)

    def post(c, slots):
        for to, slot in zip(targets[1:], slots[1:]):
            mail[c][to] = fresh[c][slot]
            mail_copy(c, to, e).start()
        inbox[c][e] = fresh[c][slots[0]]

    def last_arrivals(c, role):
        if role == 0:
            for k in range(1, dp):
                gather_copy(c, k, False).wait_recv()

    def post_wide(c, role, slots):
        last_arrivals(c, role)
        for to, slot in zip(targets[1:], slots[1:]):
            wide_mail[c][to] = wide[c][slot]
            wide_copy(c, to, e).start()
        wide_inbox[c][e] = wide[c][slots[0]]

    def deliver(c, role, taken, sources):
        for source in range(owners):
            @pl.when(e != source)
            def _():
                mail_copy(c, source, source).wait_recv()
                if EARLY(c):
                    wide_copy(c, source, source).wait_recv()

        for slot in range(new_slots):
            present = taken > slot

            def kept(value):
                return jnp.where(present, value, jnp.zeros_like(value))

            if EARLY(c):
                params[slot, rows(c)] = kept(wide_inbox[c][sources[slot]])
            else:
                params[slot, rows(c), mine] = kept(inbox[c][sources[slot], 0])
            first = 0 if EARLY(c) else 1
            for i in range(2):
                moments[i, slot, rows(c)] = kept(inbox[c][sources[slot], first + i])
        if not EARLY(c):
            gather(c, role)

    def run(role, order, slots, taken, sources, loaded):
        for kind, c, k in order:
            by_owners = kind in "UDXM" or (kind in "FW" and EARLY(c))

            def job():
                if kind in "UDX" and c not in loaded:
                    loaded.append(c)
                    g_loads[c].wait()
                if kind == "X" and "state" not in loaded:
                    loaded.append("state")
                    for load in loads:
                        load.wait()
                if kind == "U" and role == 0:
                    sum_copy(c, k, True, True).start()
                elif kind in "UD":
                    add_and_send(c, k, kind == "U")
                elif kind == "X":
                    update(c, role)
                elif kind == "M":
                    post(c, slots)
                elif kind == "F":
                    gather_copy(c, k, k < role).wait_recv()
                    gather_copy(c, k, k < role).start()
                elif kind == "W":
                    post_wide(c, role, slots)
                elif kind == "V":
                    deliver(c, role, taken, sources)
                else:
                    last_arrivals(c, role)

            if by_owners:
                pl.when(owns)(job)
            else:
                job()

    orders = [ORDERS(dp, chunks, role) for role in range(dp // 2)]
    lead = 0
    while orders[0][lead][:2] == ("U", 0):
        lead += 1
    loaded = [[] for _ in orders]

    @pl.when(place == 0)
    def _():
        run(0, orders[0][:lead], None, None, None, loaded[0])

    zero = jnp.int32(0)
    _, taken, slots, sources = lax.fori_loop(
        0, old_ref.shape[0], route, (zero, zero, (zero,) * peers, (zero,) * new_slots)
    )
    slots = tuple(jnp.minimum(slot, old_slots - 1) for slot in slots)
    sources = tuple(jnp.minimum(source, owners - 1) for source in sources)

    for role, order in enumerate(orders):
        @pl.when(place == role)
        def _():
            run(role, order[lead:] if role == 0 else order, slots, taken, sources, loaded[role])

            def gathers_sent(c):
                for k in range(dp):
                    if k <= role:
                        gather_copy(c, k, True).wait_send()
                    if k >= role > 0:
                        gather_copy(c, k, False).wait_send()

            for c in range(chunks):
                if not EARLY(c):
                    gathers_sent(c)

            @pl.when(owns)
            def _():
                for c in range(chunks):
                    if EARLY(c):
                        gathers_sent(c)
                    for k in range(dp):
                        if k != role:
                            sum_copy(c, k, k > role).wait_send()

    @pl.when(owns)
    def _():
        for c in range(chunks):
            for to in targets[1:]:
                mail_copy(c, to, e).wait_send()
                if EARLY(c):
                    wide_copy(c, to, e).wait_send()


def widen(moments, params, w_out, m_out, v_out, p_out, staged, sems, sem):
    new_slots, _, cols = w_out.shape
    z = lax.axis_index("dp")
    mine = pl.ds(pl.multiple_of(z * cols, cols), cols)
    copies = [pltpu.make_async_copy(params, p_out, sem)]
    copies[0].start()
    for slot in range(new_slots):
        parts = (params.at[slot, :, mine], moments.at[0, slot], moments.at[1, slot])
        for i, (part, out) in enumerate(zip(parts, (w_out, m_out, v_out))):
            staged[i, slot] = part[...].astype(jnp.float32)
            copies.append(pltpu.make_async_copy(staged.at[i, slot], out.at[slot], sems.at[i, slot]))
            copies[-1].start()
    for copy in copies:
        copy.wait()


def shards(grad_parts, first_moment, second_moment, master_weight, old_owner, new_owner):
    dp = lax.axis_size("dp")
    peers = lax.axis_size("expert")
    old_slots, tile_rows, cols = first_moment.shape
    owners = old_owner.shape[0] // old_slots
    new_slots = min(old_slots + old_slots // 2, peers - peers // 5)
    chunks = tile_rows // ROWS
    bf16, f32 = jnp.bfloat16, jnp.float32
    dma = pltpu.SemaphoreType.DMA
    any_space = pl.BlockSpec(memory_space=pl.ANY)
    smem = pl.BlockSpec(memory_space=pltpu.SMEM)
    vmem = pl.BlockSpec(memory_space=pltpu.VMEM)
    master = jax.ShapeDtypeStruct((new_slots, tile_rows, cols), f32)
    scratch = [
        pltpu.VMEM((old_slots, tile_rows, dp * cols), bf16),
        pltpu.VMEM((3, old_slots, tile_rows, cols), f32),
        pltpu.VMEM((dp, old_slots, tile_rows, cols), bf16),
        pltpu.VMEM((2, dp, old_slots, tile_rows, cols), bf16),
    ]
    first = [EARLY(c) for c in range(chunks)]
    kept = [2 if flag else 3 for flag in first]
    width = [dp * cols if flag else 128 for flag in first]
    scratch += [pltpu.VMEM((old_slots, n, ROWS, cols), bf16) for n in kept]
    scratch += [pltpu.VMEM((peers, n, ROWS, cols), bf16) for n in kept]
    scratch += [pltpu.VMEM((owners, n, ROWS, cols), bf16) for n in kept]
    scratch += [pltpu.VMEM((old_slots, ROWS, n), bf16) for n in width]
    scratch += [pltpu.VMEM((peers, ROWS, n), bf16) for n in width]
    scratch += [pltpu.VMEM((owners, ROWS, n), bf16) for n in width]
    scratch += [dma((chunks,)), dma((3,))] + [dma((2, chunks, dp))] * 4 + [dma((chunks, peers))] * 4
    results = new_slots * tile_rows * cols * (4 + 2 * dp)
    moments, params = pl.pallas_call(
        functools.partial(kernel, dp, peers, owners, chunks),
        out_shape=(
            pltpu.VMEM((2, new_slots, tile_rows, cols), bf16),
            pltpu.VMEM((new_slots, tile_rows, dp * cols), bf16),
        ),
        in_specs=[smem] * 2 + [any_space] * 4,
        out_specs=(vmem,) * 2,
        scratch_shapes=scratch,
        compiler_params=pltpu.CompilerParams(
            collective_id=0, has_side_effects=True, vmem_limit_bytes=67043328 - results - 2**19
        ),
    )(old_owner, new_owner, grad_parts, first_moment, second_moment, master_weight)
    return pl.pallas_call(
        widen,
        out_shape=(master,) * 3
        + (jax.ShapeDtypeStruct((new_slots, tile_rows, dp * cols), bf16),),
        in_specs=[vmem] * 2,
        out_specs=(any_space,) * 4,
        scratch_shapes=[pltpu.VMEM((3, new_slots, tile_rows, cols), f32), dma((3, new_slots)), dma],
        compiler_params=pltpu.CompilerParams(vmem_limit_bytes=2**24),
    )(moments, params)


def solution(mesh):
    placed = (
        P("dp", "expert", None, None),
        P("expert", None, "dp"),
        P("expert", None, "dp"),
        P("expert", None, "dp"),
        P(),
        P(),
    )
    return jax.shard_map(
        shards,
        mesh=mesh,
        in_specs=placed,
        out_specs=(
            P("expert", None, "dp"),
            P("expert", None, "dp"),
            P("expert", None, "dp"),
            P("expert", None, None),
        ),
        check_vma=False,
    )
```

```python
import functools
import typing

import jax
import jax.numpy as jnp
from jax import lax
from jax.experimental import pallas as pl
from jax.experimental.pallas import tpu as pltpu
from jax.sharding import PartitionSpec as P

MESH = pl.DeviceIdType.MESH
ROWS = 16
KINDS = 'UDXMWFVZ'
PARTS = (1, 1, 1, 1, 1, 1, 1, 1)
EARLY = (0, 1, 1, 1, 0, 1, 0, 0)
SPLIT = (1, 0, 0, 0, 0, 0, 0, 1)
ORDERS = (
    (
        13, 43, 2, 3, 23, 1, 12, 33, 42, 11, 2010, 41, 63, 62, 53, 3010, 73, 2040, 61, 3040, 2000, 22, 52, 2020,
        21, 3020, 51, 32, 4000, 72, 2030, 3000, 3030, 4010, 2060, 3060, 2050, 71, 3050, 2070, 4070, 31, 6000,
        6040, 6060, 4020, 6010, 6070, 4050, 4030, 6020, 3070, 6050, 6030, 7040, 7000, 7070, 7060,
    ),
    (
        13, 43, 2, 1010, 3, 23, 1040, 2000, 4000, 12, 1000, 33, 1020, 3000, 42, 6000, 2010, 3010, 1030, 5010,
        2040, 3040, 63, 5002, 62, 5012, 53, 5013, 4010, 73, 7000, 1060, 6040, 2060, 22, 1050, 52, 1070, 3060,
        5020, 5042, 2020, 3020, 2050, 3050, 32, 72, 5023, 5022, 4020, 5052, 5050, 6060, 2070, 5030, 2030, 4070,
        3070, 3030, 5053, 5000, 5062, 5033, 5040, 5032, 4030, 6070, 6010, 5070, 7070, 5043, 6020, 5060, 5072,
        4050, 5073, 5003, 5063, 6030, 6050,
    ),
)


def adam_step(gradient, moment_one, moment_two, weight):
    moment_one = 0.9 * moment_one + 0.1 * gradient
    moment_two = 0.95 * moment_two + 0.05 * gradient * gradient
    update = moment_one / (1.0 - 0.9**50) / (jnp.sqrt(moment_two / (1.0 - 0.95**50)) + 1e-08)
    weight = weight - 0.05 * (update + 0.1 * weight)
    return (weight, moment_one, moment_two)


class Chunk(typing.NamedTuple):
    row: int
    col: int
    width: int
    early: bool
    split: bool


def job_list(dp, chunks, role):
    jobs = []
    for c, chunk in enumerate(chunks):
        jobs += [("U", c, k) for k in range(dp - 1, role, -1)] + [("D", c, k) for k in range(role)] + [("X", c, 0)]
        passed = [("F", c, k) for k in range(role - 1, -1, -1)]
        if role > 0:
            passed += [("F", c, k) for k in range(role + 1, dp)]
        if chunk.early:
            jobs += [("M", c, 0)] + passed + [("W", c, 0), ("V", c, 0)]
        else:
            jobs += [("W", c, 0)] * chunk.split + [("M", c, 0), ("V", c, 0)] + passed
            jobs += [("Z", c, 0)] * (chunk.split or role == 0)
    return jobs


def plan(dp, tile_rows, cols):
    tuned = (dp == len(ORDERS) * 2) and tile_rows == ROWS * len(PARTS) and cols % (128 * max(PARTS)) == 0
    parts = PARTS if tuned else (1,) * (tile_rows // ROWS)
    spans = [(i * ROWS, j * (cols // n), cols // n) for i, n in enumerate(parts) for j in range(n)]
    chunks = [
        Chunk(*span, *((EARLY[c] == 1, SPLIT[c] == 1) if tuned else (c % 2 == 0, False)))
        for c, span in enumerate(spans)
    ]
    orders = [job_list(dp, chunks, role) for role in range(dp // 2)]
    if tuned:
        orders = [
            [(KINDS[code // 1000], code // 10 % 100, code % 10) for code in coded] for coded in ORDERS
        ]
    return chunks, orders


def kernel(dp, peers, owners, chunks, orders, old_ref, new_ref, g_hbm, m_hbm, v_hbm, w_hbm, *rest):
    moments, params, rest = rest[0], rest[1], rest[2:]
    g, state, part, line = rest[:4]
    rest = rest[4:]
    count = len(chunks)
    fresh, mail, inbox, wide, wide_mail, wide_inbox = (rest[i * count : (i + 1) * count] for i in range(6))
    (g_sem, in_sem, s_send, s_recv, a_send, a_recv, x_send, x_recv, w_send, w_recv) = rest[6 * count :]
    z = lax.axis_index("dp")
    e = lax.axis_index("expert")
    old_slots, cols = state.shape[1], state.shape[-1]
    new_slots = params.shape[0]
    far = jnp.where(z < dp // 2, 0, 1)
    place = jnp.where(z < dp // 2, z, dp - 1 - z)
    ahead = 1 - 2 * far
    owns = e < owners

    if peers & (peers - 1):
        targets = [lax.rem(e + step, peers) for step in range(peers)]
    else:
        bits = [1 << i for i in range(peers.bit_length() - 1)]
        turns = {bit: bit * (1 - 2 * lax.rem(e // bit, 2)) for bit in bits}
        targets = [e + sum(turns[bit] for bit in bits if mask & bit) for mask in (0, *range(peers - 1, 0, -1))]

    def rows(c):
        return pl.ds(chunks[c].row, ROWS)

    def span(c):
        return pl.ds(chunks[c].col, chunks[c].width)

    def real(k):
        return k + far * (dp - 1 - 2 * k)

    def block(c, k):
        return pl.ds(pl.multiple_of(real(k) * cols + chunks[c].col, 128), chunks[c].width)

    def wide_block(c, k):
        return pl.ds(pl.multiple_of(k * chunks[c].width, 128), chunks[c].width)

    def mine(c):
        return pl.ds(pl.multiple_of(z * cols + chunks[c].col, 128), chunks[c].width)

    def way(right):
        return far if right else 1 - far

    def beside(right):
        return {"dp": z + ahead if right else z - ahead}

    barrier = pltpu.get_barrier_semaphore()
    for to in targets[1:]:
        pl.semaphore_signal(barrier, inc=1, device_id={"expert": to}, device_id_type=MESH)
    for step in (-1, 1):
        @pl.when((z + step >= 0) & (z + step < dp))
        def _():
            pl.semaphore_signal(barrier, inc=1, device_id={"dp": z + step}, device_id_type=MESH)

    g_loads = [
        pltpu.make_async_copy(g_hbm.at[0, :, pl.ds(row, ROWS)], g.at[:, pl.ds(row, ROWS)], g_sem.at[row // ROWS])
        for row in range(0, g.shape[1], ROWS)
    ]
    loads = [
        pltpu.make_async_copy(ref, state.at[i], in_sem) for i, ref in enumerate((m_hbm, v_hbm, w_hbm))
    ]

    @pl.when(owns)
    def _():
        for load in g_loads[:1] + loads + g_loads[1:]:
            load.start()

    inner = (z > 0).astype(jnp.int32) + (z < dp - 1).astype(jnp.int32)
    pl.semaphore_wait(barrier, peers - 1 + inner)

    def route(tile, carry):
        sent, taken, slots, sources = carry
        old, new = old_ref[tile], new_ref[tile]
        leaves, comes = old == e, new == e
        slots = tuple(jnp.where(leaves & (new == to), sent, slot) for to, slot in zip(targets, slots))
        sources = tuple(
            jnp.where(comes & (taken == slot), old, source) for slot, source in enumerate(sources)
        )
        return sent + leaves.astype(jnp.int32), taken + comes.astype(jnp.int32), slots, sources

    def taken_by(sem, ref):
        pltpu.make_async_copy(ref, ref, sem).wait()

    def sum_copy(c, k, right, raw=False):
        src = g.at[:, rows(c), block(c, k)] if raw else part.at[real(k), :, rows(c), span(c)]
        return pltpu.make_async_remote_copy(
            src, line.at[way(right), real(k), :, rows(c), span(c)], s_send, s_recv.at[c, real(k)],
            device_id=beside(right), device_id_type=MESH,
        )

    def gather_copy(c, k, right, to_end):
        where = wide[c].at[:, :, wide_block(c, real(k))] if chunks[c].early else params.at[:, rows(c), block(c, k)]
        return pltpu.make_async_remote_copy(
            where, where, a_send.at[c], a_recv.at[c, real(0 if to_end else k)],
            device_id=beside(right), device_id_type=MESH,
        )

    def gather_send(c, k, right, role):
        gather_copy(c, k, right, role == 1 and not right).start()

    def gather_bytes(c, pieces):
        ref = g if chunks[c].early else params
        return ref.at[:, pl.ds(0, pieces * ROWS), pl.ds(0, chunks[c].width)]

    def mail_copy(c, to):
        return pltpu.make_async_remote_copy(
            mail[c].at[to], inbox[c].at[e], x_send.at[c], x_recv.at[c],
            device_id={"expert": to}, device_id_type=MESH,
        )

    def mail_bytes(c, boxes):
        return mail[c].at[pl.ds(0, boxes)]

    def weights_copy(c, to):
        return pltpu.make_async_remote_copy(
            wide_mail[c].at[to], wide_inbox[c].at[e], w_send.at[c], w_recv.at[c],
            device_id={"expert": to}, device_id_type=MESH,
        )

    def weights_bytes(c, boxes):
        return wide_mail[c].at[pl.ds(0, boxes)]

    def arrived(c, k, right):
        return line[way(right), real(k), :, rows(c), span(c)].astype(jnp.float32)

    def add_and_send(c, k, right):
        sum_copy(c, k, right).wait_recv()
        total = g[:, rows(c), block(c, k)].astype(jnp.float32) + arrived(c, k, right)
        part[real(k), :, rows(c), span(c)] = total.astype(jnp.bfloat16)
        sum_copy(c, k, right).start()

    def gather(c, role):
        gather_send(c, role, True, role)
        if role > 0:
            gather_send(c, role, False, role)

    def update(c, role):
        sides = [right for right in (True, False) if role > 0 or not right]
        at = line.at[pl.ds(0, len(sides)), z, :, rows(c), span(c)]
        taken_by(s_recv.at[c, z], at)
        for slot in range(old_slots):
            gradient = g[slot, rows(c), mine(c)].astype(jnp.float32)
            for right in sides:
                gradient += line[way(right), z, slot, rows(c), span(c)].astype(jnp.float32)
            values = adam_step(gradient, *(state[i, slot, rows(c), span(c)] for i in range(3)))
            values = [value.astype(jnp.bfloat16) for value in values]
            if chunks[c].early:
                wide[c][slot, :, wide_block(c, z)] = values.pop(0)
            elif chunks[c].split:
                wide[c][slot] = values.pop(0)
            for i, value in enumerate(values):
                fresh[c][slot, i] = value
        if chunks[c].early:
            gather(c, role)

    def post(c, slots):
        for to, slot in zip(targets[1:], slots[1:]):
            mail[c][to] = fresh[c][slot]
            mail_copy(c, to).start()
        inbox[c][e] = fresh[c][slots[0]]

    def last_arrivals(c, role):
        if role == 0:
            taken_by(a_recv.at[c, z], gather_bytes(c, dp - 1))

    def post_weights(c, role, slots):
        if chunks[c].early:
            last_arrivals(c, role)
        for to, slot in zip(targets[1:], slots[1:]):
            wide_mail[c][to] = wide[c][slot]
            weights_copy(c, to).start()
        wide_inbox[c][e] = wide[c][slots[0]]

    def receive(c, moments_too, weights_too):
        for mask, boxes in ((owns, owners - 1), (e >= owners, owners)):
            @pl.when(mask)
            def _():
                if moments_too:
                    taken_by(x_recv.at[c], mail_bytes(c, boxes))
                if weights_too:
                    taken_by(w_recv.at[c], weights_bytes(c, boxes))

    def kept(slot, taken, value):
        return jnp.where(taken > slot, value, jnp.zeros_like(value))

    def place_moments(c, taken, sources):
        first = inbox[c].shape[1] - 2
        for slot in range(new_slots):
            for i in range(2):
                moments[i, slot, rows(c), span(c)] = kept(slot, taken, inbox[c][sources[slot], first + i])

    def deliver(c, role, taken, sources):
        receive(c, not chunks[c].split, chunks[c].early or chunks[c].split)
        for slot in range(new_slots):
            if chunks[c].early:
                for k in range(dp):
                    value = wide_inbox[c][sources[slot], :, wide_block(c, k)]
                    params[slot, rows(c), pl.ds(k * cols + chunks[c].col, chunks[c].width)] = kept(slot, taken, value)
            else:
                box = wide_inbox[c][sources[slot]] if chunks[c].split else inbox[c][sources[slot], 0]
                params[slot, rows(c), mine(c)] = kept(slot, taken, box)
        if not chunks[c].early:
            gather(c, role)
        if not chunks[c].split:
            place_moments(c, taken, sources)

    def finish(c, role, taken, sources):
        if chunks[c].split:
            receive(c, True, False)
            place_moments(c, taken, sources)
        last_arrivals(c, role)

    def run(role, order, slots, taken, sources, loaded):
        for kind, c, k in order:
            by_owners = kind in "UDXMW" or (kind == "F" and chunks[c].early)

            def job():
                if kind in "UDX" and chunks[c].row not in loaded:
                    loaded.append(chunks[c].row)
                    g_loads[chunks[c].row // ROWS].wait()
                if kind == "X" and -1 not in loaded:
                    loaded.append(-1)
                    taken_by(in_sem, state)
                if kind == "U" and role == 0:
                    sum_copy(c, k, True, True).start()
                elif kind in "UD":
                    add_and_send(c, k, kind == "U")
                elif kind == "X":
                    update(c, role)
                elif kind == "M":
                    post(c, slots)
                elif kind == "F":
                    gather_copy(c, k, k < role, False).wait_recv()
                    gather_send(c, k, k < role, role)
                elif kind == "W":
                    post_weights(c, role, slots)
                elif kind == "V":
                    deliver(c, role, taken, sources)
                else:
                    finish(c, role, taken, sources)

            if by_owners:
                pl.when(owns)(job)
            else:
                job()

    lead = 0
    while orders[0][lead][:2] == ("U", 0):
        lead += 1
    loaded = [[] for _ in orders]

    @pl.when(place == 0)
    def _():
        run(0, orders[0][:lead], None, None, None, loaded[0])

    zero = jnp.int32(0)
    _, taken, slots, sources = lax.fori_loop(
        0, old_ref.shape[0], route, (zero, zero, (zero,) * peers, (zero,) * new_slots)
    )
    slots = tuple(jnp.minimum(slot, old_slots - 1) for slot in slots)
    sources = tuple(jnp.minimum(source, owners - 1) for source in sources)

    for role, order in enumerate(orders):
        @pl.when(place == role)
        def _():
            run(role, order[lead:] if role == 0 else order, slots, taken, sources, loaded[role])

            def gathers_sent(c):
                taken_by(a_send.at[c], gather_bytes(c, dp + 1 if role > 0 else 1))

            for c in range(count):
                if not chunks[c].early:
                    gathers_sent(c)

            @pl.when(owns)
            def _():
                for c in range(count):
                    if chunks[c].early:
                        gathers_sent(c)

    @pl.when(owns)
    def _():
        taken_by(s_send, part.at[pl.ds(0, dp - 1)])
        for c in range(count):
            taken_by(x_send.at[c], mail_bytes(c, peers - 1))
            if chunks[c].early or chunks[c].split:
                taken_by(w_send.at[c], weights_bytes(c, peers - 1))


def widen(moments, params, w_out, m_out, v_out, p_out, staged, sems, sem):
    new_slots, _, cols = w_out.shape
    z = lax.axis_index("dp")
    mine = pl.ds(pl.multiple_of(z * cols, cols), cols)
    copies = [pltpu.make_async_copy(params, p_out, sem)]
    copies[0].start()
    for slot in range(new_slots):
        parts = (params.at[slot, :, mine], moments.at[0, slot], moments.at[1, slot])
        for i, (part, out) in enumerate(zip(parts, (w_out, m_out, v_out))):
            staged[i, slot] = part[...].astype(jnp.float32)
            copies.append(pltpu.make_async_copy(staged.at[i, slot], out.at[slot], sems.at[i, slot]))
            copies[-1].start()
    for copy in copies:
        copy.wait()


def shards(grad_parts, first_moment, second_moment, master_weight, old_owner, new_owner):
    dp = lax.axis_size("dp")
    peers = lax.axis_size("expert")
    old_slots, tile_rows, cols = first_moment.shape
    owners = old_owner.shape[0] // old_slots
    new_slots = min(old_slots + old_slots // 2, peers - peers // 5)
    chunks, orders = plan(dp, tile_rows, cols)
    count = len(chunks)
    bf16, f32 = jnp.bfloat16, jnp.float32
    dma = pltpu.SemaphoreType.DMA
    any_space = pl.BlockSpec(memory_space=pl.ANY)
    smem = pl.BlockSpec(memory_space=pltpu.SMEM)
    vmem = pl.BlockSpec(memory_space=pltpu.VMEM)
    master = jax.ShapeDtypeStruct((new_slots, tile_rows, cols), f32)
    scratch = [
        pltpu.VMEM((old_slots, tile_rows, dp * cols), bf16),
        pltpu.VMEM((3, old_slots, tile_rows, cols), f32),
        pltpu.VMEM((dp, old_slots, tile_rows, cols), bf16),
        pltpu.VMEM((2, dp, old_slots, tile_rows, cols), bf16),
    ]
    kept = [2 if chunk.early or chunk.split else 3 for chunk in chunks]
    wide = [chunk.width * (dp if chunk.early else 1) if chunk.early or chunk.split else 128 for chunk in chunks]
    for boxes in (old_slots, peers, owners):
        scratch += [pltpu.VMEM((boxes, n, ROWS, chunk.width), bf16) for n, chunk in zip(kept, chunks)]
    for boxes in (old_slots, peers, owners):
        scratch += [pltpu.VMEM((boxes, ROWS, n), bf16) for n in wide]
    scratch += [dma((tile_rows // ROWS,)), dma, dma] + [dma((count, dp)), dma((count,)), dma((count, dp))]
    scratch += [dma((count,))] * 4
    results = new_slots * tile_rows * cols * (4 + 2 * dp)
    moments, params = pl.pallas_call(
        functools.partial(kernel, dp, peers, owners, chunks, orders),
        out_shape=(
            pltpu.VMEM((2, new_slots, tile_rows, cols), bf16),
            pltpu.VMEM((new_slots, tile_rows, dp * cols), bf16),
        ),
        in_specs=[smem] * 2 + [any_space] * 4,
        out_specs=(vmem,) * 2,
        scratch_shapes=scratch,
        compiler_params=pltpu.CompilerParams(
            collective_id=0, has_side_effects=True, vmem_limit_bytes=67043328 - results - 2**19
        ),
    )(old_owner, new_owner, grad_parts, first_moment, second_moment, master_weight)
    return pl.pallas_call(
        widen,
        out_shape=(master,) * 3
        + (jax.ShapeDtypeStruct((new_slots, tile_rows, dp * cols), bf16),),
        in_specs=[vmem] * 2,
        out_specs=(any_space,) * 4,
        scratch_shapes=[pltpu.VMEM((3, new_slots, tile_rows, cols), f32), dma((3, new_slots)), dma],
        compiler_params=pltpu.CompilerParams(vmem_limit_bytes=2**24),
    )(moments, params)


def solution(mesh):
    placed = (
        P("dp", "expert", None, None),
        P("expert", None, "dp"),
        P("expert", None, "dp"),
        P("expert", None, "dp"),
        P(),
        P(),
    )
    return jax.shard_map(
        shards,
        mesh=mesh,
        in_specs=placed,
        out_specs=(
            P("expert", None, "dp"),
            P("expert", None, "dp"),
            P("expert", None, "dp"),
            P("expert", None, None),
        ),
        check_vma=False,
    )
```

```python
import functools
import typing

import jax
import jax.numpy as jnp
from jax import lax
from jax.experimental import pallas as pl
from jax.experimental.pallas import tpu as pltpu
from jax.sharding import PartitionSpec as P

MESH = pl.DeviceIdType.MESH
ROWS = 16
KINDS = 'UDXMWFVZA'
PARTS = (2, 2, 2, 2, 2, 2, 2, 2)
EARLY = (0, 0, 0, 1, 1, 0, 1, 0, 1, 1, 0, 1, 0, 1, 1, 0)
SPLIT = (1, 1, 0, 0, 0, 0, 0, 0, 0, 0, 0, 0, 0, 0, 0, 0)
AHEAD = (0, 0, 0, 0, 0, 0, 0, 0, 0, 0, 0, 0, 0, 0, 0, 0)
ORDERS = (
    (
        32, 2, 33, 23, 123, 1, 92, 13, 73, 31, 12, 91, 93, 3, 11, 43, 22, 2030, 52, 153, 113, 21, 53, 3030,
        2020, 63, 3020, 2120, 3120, 2010, 4010, 3010, 51, 42, 122, 2070, 83, 3070, 121, 72, 2000, 41, 103, 143,
        3000, 2090, 71, 62, 4030, 133, 2040, 152, 3040, 3090, 2050, 61, 2150, 151, 2060, 2110, 3050, 82, 112,
        141, 142, 4000, 3150, 111, 4090, 132, 2140, 81, 102, 6150, 101, 6010, 3110, 4040, 131, 6050, 2100, 6030,
        6000, 6120, 2130, 6070, 2080, 3130, 3080, 6040, 3100, 3060, 3140, 4060, 6020, 6100, 4110, 4140, 6110,
        4080, 4130, 6090, 6140, 6080, 7050, 7070, 7000, 7010, 6060, 7150, 7100, 7120, 6130, 7020,
    ),
    (
        32, 2, 33, 23, 123, 2000, 4000, 1030, 92, 1020, 13, 1120, 73, 3000, 2030, 3030, 12, 6000, 93, 1010, 3,
        1070, 2090, 5032, 2010, 4010, 43, 22, 5002, 3010, 3090, 5030, 1090, 52, 1000, 153, 5092, 1040, 113,
        2020, 3020, 53, 5033, 6010, 63, 2050, 3050, 1150, 42, 1110, 122, 1050, 4030, 83, 6020, 1060, 72, 5012,
        2040, 2120, 3120, 143, 1080, 5090, 6050, 3040, 2070, 103, 5042, 62, 5022, 7000, 3070, 5093, 5040, 133,
        4090, 1140, 6120, 5060, 1100, 152, 5110, 5043, 2060, 6070, 1130, 5052, 4040, 112, 82, 2150, 5063, 142,
        3150, 5113, 5140, 3060, 5062, 2110, 2080, 5072, 4060, 132, 102, 5150, 2140, 3110, 6150, 3080, 5143,
        5122, 5112, 6030, 3140, 2130, 2100, 5050, 5130, 5142, 3100, 5000, 3130, 5082, 5010, 5153, 5080, 5132,
        5053, 4140, 5120, 5133, 6040, 5152, 5070, 5100, 5083, 5003, 6060, 4080, 4130, 6100, 4110, 5123, 5103,
        5073, 5020, 5013, 7010, 6080, 6140, 5102, 5023, 6090, 6130, 6110,
    ),
)


def moment_step(gradient, moment_one, moment_two):
    moment_one = 0.9 * moment_one + 0.1 * gradient
    moment_two = 0.95 * moment_two + 0.05 * gradient * gradient
    return moment_one, moment_two


def weight_step(moment_one, moment_two, weight):
    update = moment_one / (1.0 - 0.9**50) / (jnp.sqrt(moment_two / (1.0 - 0.95**50)) + 1e-08)
    return weight - 0.05 * (update + 0.1 * weight)


class Chunk(typing.NamedTuple):
    row: int
    col: int
    width: int
    early: bool
    split: bool
    ahead: bool


def job_list(dp, chunks, role):
    jobs = []
    for c, chunk in enumerate(chunks):
        jobs += [("U", c, k) for k in range(dp - 1, role, -1)] + [("D", c, k) for k in range(role)] + [("X", c, 0)]
        passed = [("F", c, k) for k in range(role - 1, -1, -1)]
        if role > 0:
            passed += [("F", c, k) for k in range(role + 1, dp)]
        if chunk.early:
            jobs += [("M", c, 0)] + passed + [("W", c, 0), ("V", c, 0)]
        else:
            jobs += [("A", c, 0)] * chunk.ahead + [("W", c, 0)] * chunk.split + [("M", c, 0), ("V", c, 0)] + passed
            jobs += [("Z", c, 0)] * (chunk.split or role == 0)
    return jobs


def plan(dp, tile_rows, cols):
    tuned = (dp == len(ORDERS) * 2) and tile_rows == ROWS * len(PARTS) and cols % (128 * max(PARTS)) == 0
    parts = PARTS if tuned else (1,) * (tile_rows // ROWS)
    spans = [(i * ROWS, j * (cols // n), cols // n) for i, n in enumerate(parts) for j in range(n)]
    chunks = [
        Chunk(*span, *((EARLY[c] == 1, SPLIT[c] == 1, AHEAD[c] == 1) if tuned else (c % 2 == 0, False, False)))
        for c, span in enumerate(spans)
    ]
    orders = [job_list(dp, chunks, role) for role in range(dp // 2)]
    if tuned:
        orders = [
            [(KINDS[code // 1000], code // 10 % 100, code % 10) for code in coded] for coded in ORDERS
        ]
    return chunks, orders


def kernel(dp, peers, owners, chunks, orders, old_ref, new_ref, g_hbm, m_hbm, v_hbm, w_hbm, *rest):
    moments, params, rest = rest[0], rest[1], rest[2:]
    g, state, part, line = rest[:4]
    rest = rest[4:]
    count = len(chunks)
    fresh, mail, inbox, wide, wide_mail, wide_inbox = (rest[i * count : (i + 1) * count] for i in range(6))
    (g_sem, in_sem, sent, z_recv, x_recv, w_recv) = rest[6 * count :]
    z = lax.axis_index("dp")
    e = lax.axis_index("expert")
    old_slots, cols = state.shape[1], state.shape[-1]
    new_slots = params.shape[0]
    far = jnp.where(z < dp // 2, 0, 1)
    place = jnp.where(z < dp // 2, z, dp - 1 - z)
    ahead = 1 - 2 * far
    owns = e < owners

    if peers & (peers - 1):
        targets = [lax.rem(e + step, peers) for step in range(peers)]
    else:
        bits = [1 << i for i in range(peers.bit_length() - 1)]
        turns = {bit: bit * (1 - 2 * lax.rem(e // bit, 2)) for bit in bits}
        targets = [e + sum(turns[bit] for bit in bits if mask & bit) for mask in (0, *range(peers - 1, 0, -1))]

    def rows(c):
        return pl.ds(chunks[c].row, ROWS)

    def span(c):
        return pl.ds(chunks[c].col, chunks[c].width)

    def real(k):
        return k + far * (dp - 1 - 2 * k)

    def block(c, k):
        return pl.ds(pl.multiple_of(real(k) * cols + chunks[c].col, 128), chunks[c].width)

    def wide_block(c, k):
        return pl.ds(pl.multiple_of(k * chunks[c].width, 128), chunks[c].width)

    def mine(c):
        return pl.ds(pl.multiple_of(z * cols + chunks[c].col, 128), chunks[c].width)

    def way(right):
        return far if right else 1 - far

    def beside(right):
        return {"dp": z + ahead if right else z - ahead}

    g_loads = [
        pltpu.make_async_copy(g_hbm.at[0, :, pl.ds(row, ROWS)], g.at[:, pl.ds(row, ROWS)], g_sem.at[row // ROWS])
        for row in range(0, g.shape[1], ROWS)
    ]
    loads = [pltpu.make_async_copy(ref, state.at[i], in_sem) for i, ref in enumerate((m_hbm, v_hbm, w_hbm))]

    @pl.when(owns)
    def _():
        g_loads[0].start()

    barrier = pltpu.get_barrier_semaphore()
    for to in targets[1:]:
        pl.semaphore_signal(barrier, inc=1, device_id={"expert": to}, device_id_type=MESH)
    for step in (-1, 1):
        @pl.when((z + step >= 0) & (z + step < dp))
        def _():
            pl.semaphore_signal(barrier, inc=1, device_id={"dp": z + step}, device_id_type=MESH)

    @pl.when(owns)
    def _():
        for load in loads + g_loads[1:]:
            load.start()

    inner = (z > 0).astype(jnp.int32) + (z < dp - 1).astype(jnp.int32)
    pl.semaphore_wait(barrier, peers - 1 + inner)

    def route(tile, carry):
        sent, taken, slots, sources = carry
        old, new = old_ref[tile], new_ref[tile]
        leaves, comes = old == e, new == e
        slots = tuple(jnp.where(leaves & (new == to), sent, slot) for to, slot in zip(targets, slots))
        sources = tuple(
            jnp.where(comes & (taken == slot), old, source) for slot, source in enumerate(sources)
        )
        return sent + leaves.astype(jnp.int32), taken + comes.astype(jnp.int32), slots, sources

    def taken_by(sem, ref):
        pltpu.make_async_copy(ref, ref, sem).wait()

    def sum_copy(c, k, right, raw=False):
        src = g.at[:, rows(c), block(c, k)] if raw else part.at[real(k), :, rows(c), span(c)]
        return pltpu.make_async_remote_copy(
            src, line.at[way(right), real(k), :, rows(c), span(c)], sent, z_recv.at[c, real(k)],
            device_id=beside(right), device_id_type=MESH,
        )

    def gather_copy(c, k, right, to_end):
        where = wide[c].at[:, :, wide_block(c, real(k))] if chunks[c].early else params.at[:, rows(c), block(c, k)]
        return pltpu.make_async_remote_copy(
            where, where, sent, z_recv.at[c, real(1 if to_end else k)],
            device_id=beside(right), device_id_type=MESH,
        )

    def gather_send(c, k, right, role):
        gather_copy(c, k, right, role == 1 and not right).start()

    def gather_bytes(c, pieces):
        ref = g if chunks[c].early else params
        return ref.at[:, pl.ds(0, pieces * ROWS), pl.ds(0, chunks[c].width)]

    def mail_copy(c, to):
        return pltpu.make_async_remote_copy(
            mail[c].at[to], inbox[c].at[e], sent, x_recv.at[c],
            device_id={"expert": to}, device_id_type=MESH,
        )

    def mail_bytes(c, boxes):
        return mail[c].at[pl.ds(0, boxes)]

    def weights_copy(c, to):
        return pltpu.make_async_remote_copy(
            wide_mail[c].at[to], wide_inbox[c].at[e], sent, w_recv.at[c],
            device_id={"expert": to}, device_id_type=MESH,
        )

    def weights_bytes(c, boxes):
        return wide_mail[c].at[pl.ds(0, boxes)]

    def arrived(c, k, right):
        return line[way(right), real(k), :, rows(c), span(c)].astype(jnp.float32)

    def add_and_send(c, k, right):
        sum_copy(c, k, right).wait_recv()
        total = g[:, rows(c), block(c, k)].astype(jnp.float32) + arrived(c, k, right)
        part[real(k), :, rows(c), span(c)] = total.astype(jnp.bfloat16)
        sum_copy(c, k, right).start()

    def gather(c, role):
        gather_send(c, role, True, role)
        if role > 0:
            gather_send(c, role, False, role)

    def update(c, role):
        sides = [right for right in (True, False) if role > 0 or not right]
        at = line.at[pl.ds(0, len(sides)), z, :, rows(c), span(c)]
        taken_by(z_recv.at[c, z], at)
        for slot in range(old_slots):
            gradient = g[slot, rows(c), mine(c)].astype(jnp.float32)
            for right in sides:
                gradient += line[way(right), z, slot, rows(c), span(c)].astype(jnp.float32)
            values = list(moment_step(gradient, *(state[i, slot, rows(c), span(c)] for i in range(2))))
            if not chunks[c].ahead:
                values.insert(0, weight_step(*values, state[2, slot, rows(c), span(c)]))
            values = [value.astype(jnp.bfloat16) for value in values]
            if chunks[c].early:
                wide[c][slot, :, wide_block(c, z)] = values.pop(0)
            elif chunks[c].split:
                wide[c][slot] = values.pop(0)
            for i, value in enumerate(values):
                fresh[c][slot, i] = value
        if chunks[c].early:
            gather(c, role)

    def post(c, slots):
        for to, slot in zip(targets[1:], slots[1:]):
            mail[c][to] = fresh[c][slot]
            mail_copy(c, to).start()
        inbox[c][e] = fresh[c][slots[0]]

    def last_arrivals(c, role):
        if role == 0:
            taken_by(z_recv.at[c, real(1)], gather_bytes(c, dp - 1))

    def post_old_weights(c, slots):
        for to, slot in zip(targets[1:], slots[1:]):
            wide_mail[c][to] = state[2, slot, rows(c), span(c)].astype(jnp.bfloat16)
            weights_copy(c, to).start()
        wide_inbox[c][e] = state[2, slots[0], rows(c), span(c)].astype(jnp.bfloat16)

    def post_weights(c, role, slots):
        if chunks[c].early:
            last_arrivals(c, role)
        for to, slot in zip(targets[1:], slots[1:]):
            wide_mail[c][to] = wide[c][slot]
            weights_copy(c, to).start()
        wide_inbox[c][e] = wide[c][slots[0]]

    def receive(c, moments_too, weights_too):
        for mask, boxes in ((owns, owners - 1), (e >= owners, owners)):
            @pl.when(mask)
            def _():
                if moments_too:
                    taken_by(x_recv.at[c], mail_bytes(c, boxes))
                if weights_too:
                    taken_by(w_recv.at[c], weights_bytes(c, boxes))

    def kept(slot, taken, value):
        return jnp.where(taken > slot, value, jnp.zeros_like(value))

    def place_moments(c, taken, sources):
        first = inbox[c].shape[1] - 2
        for slot in range(new_slots):
            for i in range(2):
                moments[i, slot, rows(c), span(c)] = kept(slot, taken, inbox[c][sources[slot], first + i])

    def deliver(c, role, taken, sources):
        receive(c, not chunks[c].split, chunks[c].early or chunks[c].split or chunks[c].ahead)
        for slot in range(new_slots):
            if chunks[c].early:
                for k in range(dp):
                    value = wide_inbox[c][sources[slot], :, wide_block(c, k)]
                    params[slot, rows(c), pl.ds(k * cols + chunks[c].col, chunks[c].width)] = kept(slot, taken, value)
            else:
                if chunks[c].ahead:
                    values = [inbox[c][sources[slot], i] for i in range(2)] + [wide_inbox[c][sources[slot]]]
                    box = weight_step(*(value.astype(jnp.float32) for value in values)).astype(jnp.bfloat16)
                elif chunks[c].split:
                    box = wide_inbox[c][sources[slot]]
                else:
                    box = inbox[c][sources[slot], 0]
                params[slot, rows(c), mine(c)] = kept(slot, taken, box)
        if not chunks[c].early:
            gather(c, role)
        if not chunks[c].split:
            place_moments(c, taken, sources)

    def finish(c, role, taken, sources):
        if chunks[c].split:
            receive(c, True, False)
            place_moments(c, taken, sources)
        last_arrivals(c, role)

    def run(role, order, slots, taken, sources, loaded):
        for kind, c, k in order:
            by_owners = kind in "UDXMWA" or (kind == "F" and chunks[c].early)

            def job():
                if kind in "UDX" and chunks[c].row not in loaded:
                    loaded.append(chunks[c].row)
                    g_loads[chunks[c].row // ROWS].wait()
                if kind in "XA" and -1 not in loaded:
                    loaded.append(-1)
                    taken_by(in_sem, state)
                if kind == "U" and role == 0:
                    sum_copy(c, k, True, True).start()
                elif kind in "UD":
                    add_and_send(c, k, kind == "U")
                elif kind == "X":
                    update(c, role)
                elif kind == "A":
                    post_old_weights(c, slots)
                elif kind == "M":
                    post(c, slots)
                elif kind == "F":
                    gather_copy(c, k, k < role, False).wait_recv()
                    gather_send(c, k, k < role, role)
                elif kind == "W":
                    post_weights(c, role, slots)
                elif kind == "V":
                    deliver(c, role, taken, sources)
                else:
                    finish(c, role, taken, sources)

            if by_owners:
                pl.when(owns)(job)
            else:
                job()

    lead = 0
    while orders[0][lead][:2] == ("U", 0):
        lead += 1
    loaded = [[] for _ in orders]

    @pl.when(place == 0)
    def _():
        run(0, orders[0][:lead], None, None, None, loaded[0])

    zero = jnp.int32(0)
    _, taken, slots, sources = lax.fori_loop(
        0, old_ref.shape[0], route, (zero, zero, (zero,) * peers, (zero,) * new_slots)
    )
    slots = tuple(jnp.minimum(slot, old_slots - 1) for slot in slots)
    sources = tuple(jnp.minimum(source, owners - 1) for source in sources)

    for role, order in enumerate(orders):
        @pl.when(place == role)
        def _():
            run(role, order[lead:] if role == 0 else order, slots, taken, sources, loaded[role])

            def gathers_sent(c):
                taken_by(sent, gather_bytes(c, dp + 1 if role > 0 else 1))

            for c in range(count):
                if not chunks[c].early:
                    gathers_sent(c)

            @pl.when(owns)
            def _():
                for c in range(count):
                    if chunks[c].early:
                        gathers_sent(c)

    @pl.when(owns)
    def _():
        taken_by(sent, part.at[pl.ds(0, dp - 1)])
        for c in range(count):
            taken_by(sent, mail_bytes(c, peers - 1))
            if chunks[c].early or chunks[c].split or chunks[c].ahead:
                taken_by(sent, weights_bytes(c, peers - 1))


def widen(moments, params, w_out, m_out, v_out, p_out, staged, sems):
    new_slots, _, cols = w_out.shape
    z = lax.axis_index("dp")
    mine = pl.ds(pl.multiple_of(z * cols, cols), cols)
    pltpu.make_async_copy(params, p_out, sems.at[3]).start()
    for slot in range(new_slots):
        parts = (params.at[slot, :, mine], moments.at[0, slot], moments.at[1, slot])
        for i, (part, out) in enumerate(zip(parts, (w_out, m_out, v_out))):
            staged[i, slot] = part[...].astype(jnp.float32)
            pltpu.make_async_copy(staged.at[i, slot], out.at[slot], sems.at[i]).start()
    for i, out in enumerate((w_out, m_out, v_out, p_out)):
        pltpu.make_async_copy(out, out, sems.at[i]).wait()


def shards(grad_parts, first_moment, second_moment, master_weight, old_owner, new_owner):
    dp = lax.axis_size("dp")
    peers = lax.axis_size("expert")
    old_slots, tile_rows, cols = first_moment.shape
    owners = old_owner.shape[0] // old_slots
    new_slots = min(old_slots + old_slots // 2, peers - peers // 5)
    chunks, orders = plan(dp, tile_rows, cols)
    count = len(chunks)
    bf16, f32 = jnp.bfloat16, jnp.float32
    dma = pltpu.SemaphoreType.DMA
    any_space = pl.BlockSpec(memory_space=pl.ANY)
    smem = pl.BlockSpec(memory_space=pltpu.SMEM)
    vmem = pl.BlockSpec(memory_space=pltpu.VMEM)
    master = jax.ShapeDtypeStruct((new_slots, tile_rows, cols), f32)
    scratch = [
        pltpu.VMEM((old_slots, tile_rows, dp * cols), bf16),
        pltpu.VMEM((3, old_slots, tile_rows, cols), f32),
        pltpu.VMEM((dp, old_slots, tile_rows, cols), bf16),
        pltpu.VMEM((2, dp, old_slots, tile_rows, cols), bf16),
    ]
    apart = [chunk.early or chunk.split or chunk.ahead for chunk in chunks]
    kept = [2 if flag else 3 for flag in apart]
    wide = [chunk.width * (dp if chunk.early else 1) if flag else 128 for flag, chunk in zip(apart, chunks)]
    for boxes in (old_slots, peers, owners):
        scratch += [pltpu.VMEM((boxes, n, ROWS, chunk.width), bf16) for n, chunk in zip(kept, chunks)]
    for boxes in (old_slots, peers, owners):
        scratch += [pltpu.VMEM((boxes, ROWS, n), bf16) for n in wide]
    scratch += [dma((tile_rows // ROWS,)), dma, dma, dma((count, dp))]
    scratch += [dma((count,))] * 2
    results = new_slots * tile_rows * cols * (4 + 2 * dp)
    moments, params = pl.pallas_call(
        functools.partial(kernel, dp, peers, owners, chunks, orders),
        out_shape=(
            pltpu.VMEM((2, new_slots, tile_rows, cols), bf16),
            pltpu.VMEM((new_slots, tile_rows, dp * cols), bf16),
        ),
        in_specs=[smem] * 2 + [any_space] * 4,
        out_specs=(vmem,) * 2,
        scratch_shapes=scratch,
        compiler_params=pltpu.CompilerParams(
            collective_id=0, has_side_effects=True, vmem_limit_bytes=67043328 - results - 2**19
        ),
    )(old_owner, new_owner, grad_parts, first_moment, second_moment, master_weight)
    return pl.pallas_call(
        widen,
        out_shape=(master,) * 3
        + (jax.ShapeDtypeStruct((new_slots, tile_rows, dp * cols), bf16),),
        in_specs=[vmem] * 2,
        out_specs=(any_space,) * 4,
        scratch_shapes=[pltpu.VMEM((3, new_slots, tile_rows, cols), f32), dma((4,))],
        compiler_params=pltpu.CompilerParams(vmem_limit_bytes=2**24),
    )(moments, params)


def solution(mesh):
    placed = (
        P("dp", "expert", None, None),
        P("expert", None, "dp"),
        P("expert", None, "dp"),
        P("expert", None, "dp"),
        P(),
        P(),
    )
    return jax.shard_map(
        shards,
        mesh=mesh,
        in_specs=placed,
        out_specs=(
            P("expert", None, "dp"),
            P("expert", None, "dp"),
            P("expert", None, "dp"),
            P("expert", None, None),
        ),
        check_vma=False,
    )
```

```python
import functools
import typing

import jax
import jax.numpy as jnp
from jax import lax
from jax.experimental import pallas as pl
from jax.experimental.pallas import tpu as pltpu
from jax.sharding import PartitionSpec as P

MESH = pl.DeviceIdType.MESH
ROWS = 16
KINDS = 'UDXMWFVZA'
PARTS = (2, 2, 2, 1, 1, 1, 1, 1)
EARLY = (0, 0, 1, 0, 1, 1, 1, 1, 0, 1, 0)
SPLIT = (0, 0, 0, 0, 0, 0, 0, 0, 0, 0, 0)
AHEAD = (0, 1, 0, 0, 0, 0, 0, 0, 1, 0, 1)
ORDERS = (
    (
        12, 23, 8080, 43, 22, 8010, 3, 11, 8100, 33, 13, 2, 21, 42, 53, 63, 1, 41, 2020, 2040, 3020, 3040, 32,
        2000, 62, 2030, 73, 3030, 31, 3000, 61, 2050, 52, 3050, 83, 82, 2010, 51, 3010, 2060, 81, 103, 3060, 93,
        4020, 4040, 72, 92, 2070, 3070, 71, 91, 6030, 6020, 6000, 2080, 102, 3080, 4050, 6010, 2100, 3100, 2090,
        4060, 101, 6040, 6050, 3090, 6080, 6100, 4070, 4090, 7000, 6070, 7010, 7030, 6060, 6090, 7080, 7100,
    ),
    (
        12, 8010, 23, 43, 3, 22, 8100, 2010, 3010, 33, 1020, 1040, 13, 1000, 2, 2020, 42, 1030, 53, 3020, 1010,
        6010, 5022, 63, 8080, 2000, 3000, 2040, 5040, 1050, 5012, 3040, 32, 5020, 1060, 62, 5042, 5043, 4040,
        6000, 73, 2030, 3030, 5023, 2060, 52, 5050, 5002, 3060, 83, 1070, 4020, 82, 6030, 2050, 3050, 5053,
        5060, 1080, 5062, 2080, 103, 3080, 5032, 93, 6020, 5052, 5063, 4060, 72, 1100, 4050, 92, 1090, 5070,
        6080, 2090, 6040, 3090, 5073, 2070, 6060, 102, 3070, 5030, 5082, 5090, 5072, 2100, 5092, 3100, 5000,
        5033, 5010, 4070, 5080, 5093, 5003, 4090, 5013, 5100, 6100, 5083, 6050, 5103, 5102, 6070, 6090,
    ),
)


def moment_step(gradient, moment_one, moment_two):
    moment_one = 0.9 * moment_one + 0.1 * gradient
    moment_two = 0.95 * moment_two + 0.05 * gradient * gradient
    return moment_one, moment_two


def weight_step(moment_one, moment_two, weight):
    update = moment_one / (1.0 - 0.9**50) / (jnp.sqrt(moment_two / (1.0 - 0.95**50)) + 1e-08)
    return weight - 0.05 * (update + 0.1 * weight)


class Chunk(typing.NamedTuple):
    row: int
    col: int
    width: int
    early: bool
    split: bool
    ahead: bool


def job_list(dp, chunks, role):
    jobs = []
    for c, chunk in enumerate(chunks):
        jobs += [("U", c, k) for k in range(dp - 1, role, -1)] + [("D", c, k) for k in range(role)] + [("X", c, 0)]
        passed = [("F", c, k) for k in range(role - 1, -1, -1)]
        if role > 0:
            passed += [("F", c, k) for k in range(role + 1, dp)]
        if chunk.early:
            jobs += [("A", c, 0)] * chunk.ahead + [("M", c, 0)] + passed + [("W", c, 0), ("V", c, 0)]
        else:
            jobs += [("A", c, 0)] * chunk.ahead + [("W", c, 0)] * chunk.split + [("M", c, 0), ("V", c, 0)] + passed
            jobs += [("Z", c, 0)] * (chunk.split or role == 0)
    return jobs


def plan(dp, tile_rows, cols):
    tuned = (dp == len(ORDERS) * 2) and tile_rows == ROWS * len(PARTS) and cols % (128 * max(PARTS)) == 0
    parts = PARTS if tuned else (1,) * (tile_rows // ROWS)
    spans = [(i * ROWS, j * (cols // n), cols // n) for i, n in enumerate(parts) for j in range(n)]
    chunks = [
        Chunk(*span, *((EARLY[c] == 1, SPLIT[c] == 1, AHEAD[c] == 1) if tuned else (c % 2 == 0, False, False)))
        for c, span in enumerate(spans)
    ]
    orders = [job_list(dp, chunks, role) for role in range(dp // 2)]
    if tuned:
        orders = [
            [(KINDS[code // 1000], code // 10 % 100, code % 10) for code in coded] for coded in ORDERS
        ]
    return chunks, orders


def kernel(dp, peers, owners, chunks, orders, old_ref, new_ref, g_hbm, m_hbm, v_hbm, w_hbm, *rest):
    moments, params, rest = rest[0], rest[1], rest[2:]
    g, state, part, line = rest[:4]
    rest = rest[4:]
    count = len(chunks)
    fresh, mail, inbox, wide, wide_mail, wide_inbox, old_mail, old_inbox = (
        rest[i * count : (i + 1) * count] for i in range(8)
    )
    g_sem, in_sem, sent, z_recv, x_recv, w_recv, o_recv = rest[8 * count :]
    z = lax.axis_index("dp")
    e = lax.axis_index("expert")
    old_slots, cols = state.shape[1], state.shape[-1]
    new_slots = params.shape[0]
    far = jnp.where(z < dp // 2, 0, 1)
    place = jnp.where(z < dp // 2, z, dp - 1 - z)
    ahead = 1 - 2 * far
    owns = e < owners

    if peers & (peers - 1):
        targets = [lax.rem(e + step, peers) for step in range(peers)]
    else:
        bits = [1 << i for i in range(peers.bit_length() - 1)]
        turns = {bit: bit * (1 - 2 * lax.rem(e // bit, 2)) for bit in bits}
        targets = [e + sum(turns[bit] for bit in bits if mask & bit) for mask in (0, *range(peers - 1, 0, -1))]

    def rows(c):
        return pl.ds(chunks[c].row, ROWS)

    def span(c):
        return pl.ds(chunks[c].col, chunks[c].width)

    def real(k):
        return k + far * (dp - 1 - 2 * k)

    def block(c, k):
        return pl.ds(pl.multiple_of(real(k) * cols + chunks[c].col, 128), chunks[c].width)

    def wide_block(c, k, plane):
        return pl.ds(pl.multiple_of(lax.rem(k - plane + dp, dp) * chunks[c].width, 128), chunks[c].width)

    def mine(c):
        return pl.ds(pl.multiple_of(z * cols + chunks[c].col, 128), chunks[c].width)

    def way(right):
        return far if right else 1 - far

    def beside(right):
        return {"dp": z + ahead if right else z - ahead}

    g_loads = [
        pltpu.make_async_copy(g_hbm.at[0, :, pl.ds(row, ROWS)], g.at[:, pl.ds(row, ROWS)], g_sem.at[row // ROWS])
        for row in range(0, g.shape[1], ROWS)
    ]
    loads = [pltpu.make_async_copy(ref, state.at[i], in_sem) for i, ref in enumerate((m_hbm, v_hbm, w_hbm))]

    @pl.when(owns)
    def _():
        g_loads[0].start()

    barrier = pltpu.get_barrier_semaphore()
    for to in targets[1:]:
        pl.semaphore_signal(barrier, inc=1, device_id={"expert": to}, device_id_type=MESH)
    for step in (-1, 1):
        @pl.when((z + step >= 0) & (z + step < dp))
        def _():
            pl.semaphore_signal(barrier, inc=1, device_id={"dp": z + step}, device_id_type=MESH)

    @pl.when(owns)
    def _():
        for load in loads + g_loads[1:]:
            load.start()

    inner = (z > 0).astype(jnp.int32) + (z < dp - 1).astype(jnp.int32)
    pl.semaphore_wait(barrier, peers - 1 + inner)

    def route(tile, carry):
        sent, taken, slots, sources = carry
        old, new = old_ref[tile], new_ref[tile]
        leaves, comes = old == e, new == e
        slots = tuple(jnp.where(leaves & (new == to), sent, slot) for to, slot in zip(targets, slots))
        sources = tuple(
            jnp.where(comes & (taken == slot), old, source) for slot, source in enumerate(sources)
        )
        return sent + leaves.astype(jnp.int32), taken + comes.astype(jnp.int32), slots, sources

    def taken_by(sem, ref):
        pltpu.make_async_copy(ref, ref, sem).wait()

    def sum_copy(c, k, right, raw=False):
        src = g.at[:, rows(c), block(c, k)] if raw else part.at[real(k), :, rows(c), span(c)]
        return pltpu.make_async_remote_copy(
            src, line.at[way(right), real(k), :, rows(c), span(c)], sent, z_recv.at[c, real(k)],
            device_id=beside(right), device_id_type=MESH,
        )

    def gather_copy(c, k, right, to_end):
        src = dst = params.at[:, rows(c), block(c, k)]
        if chunks[c].early:
            src = wide[c].at[:, :, wide_block(c, real(k), z)]
            dst = wide[c].at[:, :, wide_block(c, real(k), beside(right)["dp"])]
        return pltpu.make_async_remote_copy(
            src, dst, sent, z_recv.at[c, real(1 if to_end else k)],
            device_id=beside(right), device_id_type=MESH,
        )

    def gather_send(c, k, right, role):
        gather_copy(c, k, right, role == 1 and not right).start()

    def gather_bytes(c, pieces):
        ref = g if chunks[c].early else params
        return ref.at[:, pl.ds(0, pieces * ROWS), pl.ds(0, chunks[c].width)]

    def mail_copy(c, to):
        return pltpu.make_async_remote_copy(
            mail[c].at[to], inbox[c].at[e], sent, x_recv.at[c],
            device_id={"expert": to}, device_id_type=MESH,
        )

    def mail_bytes(c, boxes):
        return mail[c].at[pl.ds(0, boxes)]

    def weights_copy(c, to):
        return pltpu.make_async_remote_copy(
            wide_mail[c].at[to], wide_inbox[c].at[e], sent, w_recv.at[c],
            device_id={"expert": to}, device_id_type=MESH,
        )

    def old_copy(c, to):
        return pltpu.make_async_remote_copy(
            old_mail[c].at[to], old_inbox[c].at[e], sent, o_recv.at[c],
            device_id={"expert": to}, device_id_type=MESH,
        )

    def weights_bytes(c, boxes):
        return wide_mail[c].at[pl.ds(0, boxes)]

    def arrived(c, k, right):
        return line[way(right), real(k), :, rows(c), span(c)].astype(jnp.float32)

    def add_and_send(c, k, right):
        sum_copy(c, k, right).wait_recv()
        total = g[:, rows(c), block(c, k)].astype(jnp.float32) + arrived(c, k, right)
        part[real(k), :, rows(c), span(c)] = total.astype(jnp.bfloat16)
        sum_copy(c, k, right).start()

    def gather(c, role):
        gather_send(c, role, True, role)
        if role > 0:
            gather_send(c, role, False, role)

    def update(c, role):
        sides = [right for right in (True, False) if role > 0 or not right]
        at = line.at[pl.ds(0, len(sides)), z, :, rows(c), span(c)]
        taken_by(z_recv.at[c, z], at)
        for slot in range(old_slots):
            gradient = g[slot, rows(c), mine(c)].astype(jnp.float32)
            for right in sides:
                gradient += line[way(right), z, slot, rows(c), span(c)].astype(jnp.float32)
            values = list(moment_step(gradient, *(state[i, slot, rows(c), span(c)] for i in range(2))))
            if chunks[c].early or not chunks[c].ahead:
                values.insert(0, weight_step(*values, state[2, slot, rows(c), span(c)]))
            values = [value.astype(jnp.bfloat16) for value in values]
            if chunks[c].early:
                wide[c][slot, :, pl.ds(0, chunks[c].width)] = values.pop(0)
            elif chunks[c].split:
                wide[c][slot] = values.pop(0)
            for i, value in enumerate(values):
                fresh[c][slot, i] = value
        if chunks[c].early:
            gather(c, role)

    def post(c, slots):
        for to, slot in zip(targets[1:], slots[1:]):
            mail[c][to] = fresh[c][slot]
            mail_copy(c, to).start()
        inbox[c][e] = fresh[c][slots[0]]

    def last_arrivals(c, role):
        if role == 0:
            taken_by(z_recv.at[c, real(1)], gather_bytes(c, dp - 1))

    def post_old_weights(c, slots):
        for to, slot in zip(targets[1:], slots[1:]):
            old_mail[c][to] = state[2, slot, rows(c), span(c)].astype(jnp.bfloat16)
            old_copy(c, to).start()
        old_inbox[c][e] = state[2, slots[0], rows(c), span(c)].astype(jnp.bfloat16)

    def post_weights(c, role, slots):
        if chunks[c].early:
            last_arrivals(c, role)
        size = wide_mail[c].shape[2]
        columns = pl.ds(wide[c].shape[2] - size, size)
        for to, slot in zip(targets[1:], slots[1:]):
            wide_mail[c][to] = wide[c][slot, :, columns]
            weights_copy(c, to).start()
        wide_inbox[c][e] = wide[c][slots[0], :, columns]

    def receive(c, moments_too, weights_too, old_too):
        for mask, boxes in ((owns, owners - 1), (e >= owners, owners)):
            @pl.when(mask)
            def _():
                if moments_too:
                    taken_by(x_recv.at[c], mail_bytes(c, boxes))
                if weights_too:
                    taken_by(w_recv.at[c], weights_bytes(c, boxes))
                if old_too:
                    taken_by(o_recv.at[c], old_mail[c].at[pl.ds(0, boxes)])

    def kept(slot, taken, value):
        return jnp.where(taken > slot, value, jnp.zeros_like(value))

    def place_moments(c, taken, sources):
        first = inbox[c].shape[1] - 2
        for slot in range(new_slots):
            for i in range(2):
                moments[i, slot, rows(c), span(c)] = kept(slot, taken, inbox[c][sources[slot], first + i])

    def deliver(c, role, taken, sources):
        width = chunks[c].width
        receive(c, not chunks[c].split, chunks[c].early or chunks[c].split, chunks[c].ahead)
        for slot in range(new_slots):
            if chunks[c].ahead:
                values = [inbox[c][sources[slot], i] for i in range(2)] + [old_inbox[c][sources[slot]]]
                own = weight_step(*(value.astype(jnp.float32) for value in values)).astype(jnp.bfloat16)
            elif chunks[c].early:
                own = wide_inbox[c][sources[slot], :, pl.ds(0, width)]
            else:
                own = wide_inbox[c][sources[slot]] if chunks[c].split else inbox[c][sources[slot], 0]
            params[slot, rows(c), mine(c)] = kept(slot, taken, own)
            for step in range(1, dp if chunks[c].early else 1):
                column = pl.multiple_of(lax.rem(z + step, dp) * cols + chunks[c].col, 128)
                first = (step - 1 if chunks[c].ahead else step) * width
                value = wide_inbox[c][sources[slot], :, pl.ds(first, width)]
                params[slot, rows(c), pl.ds(column, width)] = kept(slot, taken, value)
        if not chunks[c].early:
            gather(c, role)
        if not chunks[c].split:
            place_moments(c, taken, sources)

    def finish(c, role, taken, sources):
        if chunks[c].split:
            receive(c, True, False, False)
            place_moments(c, taken, sources)
        last_arrivals(c, role)

    def run(role, order, slots, taken, sources, loaded):
        for kind, c, k in order:
            by_owners = kind in "UDXMWA" or (kind == "F" and chunks[c].early)

            def job():
                if kind in "UDX" and chunks[c].row not in loaded:
                    loaded.append(chunks[c].row)
                    g_loads[chunks[c].row // ROWS].wait()
                if kind in "XA" and -1 not in loaded:
                    loaded.append(-1)
                    taken_by(in_sem, state)
                if kind == "U" and role == 0:
                    sum_copy(c, k, True, True).start()
                elif kind in "UD":
                    add_and_send(c, k, kind == "U")
                elif kind == "X":
                    update(c, role)
                elif kind == "A":
                    post_old_weights(c, slots)
                elif kind == "M":
                    post(c, slots)
                elif kind == "F":
                    gather_copy(c, k, k < role, False).wait_recv()
                    gather_send(c, k, k < role, role)
                elif kind == "W":
                    post_weights(c, role, slots)
                elif kind == "V":
                    deliver(c, role, taken, sources)
                else:
                    finish(c, role, taken, sources)

            if by_owners:
                pl.when(owns)(job)
            else:
                job()

    lead = 0
    while orders[0][lead][:2] == ("U", 0):
        lead += 1
    loaded = [[] for _ in orders]

    @pl.when(place == 0)
    def _():
        run(0, orders[0][:lead], None, None, None, loaded[0])

    zero = jnp.int32(0)
    _, taken, slots, sources = lax.fori_loop(
        0, old_ref.shape[0], route, (zero, zero, (zero,) * peers, (zero,) * new_slots)
    )
    slots = tuple(jnp.minimum(slot, old_slots - 1) for slot in slots)
    sources = tuple(jnp.minimum(source, owners - 1) for source in sources)

    for role, order in enumerate(orders):
        @pl.when(place == role)
        def _():
            run(role, order[lead:] if role == 0 else order, slots, taken, sources, loaded[role])

            def gathers_sent(c):
                taken_by(sent, gather_bytes(c, dp + 1 if role > 0 else 1))

            for c in range(count):
                if not chunks[c].early:
                    gathers_sent(c)

            @pl.when(owns)
            def _():
                for c in range(count):
                    if chunks[c].early:
                        gathers_sent(c)

    @pl.when(owns)
    def _():
        taken_by(sent, part.at[pl.ds(0, dp - 1)])
        for c in range(count):
            taken_by(sent, mail_bytes(c, peers - 1))
            if chunks[c].early or chunks[c].split:
                taken_by(sent, weights_bytes(c, peers - 1))
            if chunks[c].ahead:
                taken_by(sent, old_mail[c].at[pl.ds(0, peers - 1)])


def widen(moments, params, w_out, m_out, v_out, p_out, staged, sems):
    new_slots, _, cols = w_out.shape
    z = lax.axis_index("dp")
    mine = pl.ds(pl.multiple_of(z * cols, cols), cols)
    pltpu.make_async_copy(params, p_out, sems.at[3]).start()
    for slot in range(new_slots):
        parts = (params.at[slot, :, mine], moments.at[0, slot], moments.at[1, slot])
        for i, (part, out) in enumerate(zip(parts, (w_out, m_out, v_out))):
            staged[i, slot] = part[...].astype(jnp.float32)
            pltpu.make_async_copy(staged.at[i, slot], out.at[slot], sems.at[i]).start()
    for i, out in enumerate((w_out, m_out, v_out, p_out)):
        pltpu.make_async_copy(out, out, sems.at[i]).wait()


def shards(grad_parts, first_moment, second_moment, master_weight, old_owner, new_owner):
    dp = lax.axis_size("dp")
    peers = lax.axis_size("expert")
    old_slots, tile_rows, cols = first_moment.shape
    owners = old_owner.shape[0] // old_slots
    new_slots = min(old_slots + old_slots // 2, peers - peers // 5)
    chunks, orders = plan(dp, tile_rows, cols)
    count = len(chunks)
    bf16, f32 = jnp.bfloat16, jnp.float32
    dma = pltpu.SemaphoreType.DMA
    any_space = pl.BlockSpec(memory_space=pl.ANY)
    smem = pl.BlockSpec(memory_space=pltpu.SMEM)
    vmem = pl.BlockSpec(memory_space=pltpu.VMEM)
    master = jax.ShapeDtypeStruct((new_slots, tile_rows, cols), f32)
    scratch = [
        pltpu.VMEM((old_slots, tile_rows, dp * cols), bf16),
        pltpu.VMEM((3, old_slots, tile_rows, cols), f32),
        pltpu.VMEM((dp, old_slots, tile_rows, cols), bf16),
        pltpu.VMEM((2, dp, old_slots, tile_rows, cols), bf16),
    ]
    kept = [2 if chunk.early or chunk.split or chunk.ahead else 3 for chunk in chunks]
    wide = [chunk.width * (dp if chunk.early else 1) if chunk.early or chunk.split else 128 for chunk in chunks]
    sent = [size - chunk.width if chunk.early and chunk.ahead else size for size, chunk in zip(wide, chunks)]
    old = [chunk.width if chunk.ahead else 128 for chunk in chunks]
    for boxes in (old_slots, peers, owners):
        scratch += [pltpu.VMEM((boxes, n, ROWS, chunk.width), bf16) for n, chunk in zip(kept, chunks)]
    for boxes, sizes in ((old_slots, wide), (peers, sent), (owners, sent), (peers, old), (owners, old)):
        scratch += [pltpu.VMEM((boxes, ROWS, n), bf16) for n in sizes]
    scratch += [dma((tile_rows // ROWS,)), dma, dma, dma((count, dp))]
    scratch += [dma((count,))] * 3
    results = new_slots * tile_rows * cols * (4 + 2 * dp)
    moments, params = pl.pallas_call(
        functools.partial(kernel, dp, peers, owners, chunks, orders),
        out_shape=(
            pltpu.VMEM((2, new_slots, tile_rows, cols), bf16),
            pltpu.VMEM((new_slots, tile_rows, dp * cols), bf16),
        ),
        in_specs=[smem] * 2 + [any_space] * 4,
        out_specs=(vmem,) * 2,
        scratch_shapes=scratch,
        compiler_params=pltpu.CompilerParams(
            collective_id=0, has_side_effects=True, vmem_limit_bytes=67043328 - results - 2**19
        ),
    )(old_owner, new_owner, grad_parts, first_moment, second_moment, master_weight)
    return pl.pallas_call(
        widen,
        out_shape=(master,) * 3
        + (jax.ShapeDtypeStruct((new_slots, tile_rows, dp * cols), bf16),),
        in_specs=[vmem] * 2,
        out_specs=(any_space,) * 4,
        scratch_shapes=[pltpu.VMEM((3, new_slots, tile_rows, cols), f32), dma((4,))],
        compiler_params=pltpu.CompilerParams(vmem_limit_bytes=2**24),
    )(moments, params)


def solution(mesh):
    placed = (
        P("dp", "expert", None, None),
        P("expert", None, "dp"),
        P("expert", None, "dp"),
        P("expert", None, "dp"),
        P(),
        P(),
    )
    return jax.shard_map(
        shards,
        mesh=mesh,
        in_specs=placed,
        out_specs=(
            P("expert", None, "dp"),
            P("expert", None, "dp"),
            P("expert", None, "dp"),
            P("expert", None, None),
        ),
        check_vma=False,
    )
```

```python
import functools
import typing

import jax
import jax.numpy as jnp
from jax import lax
from jax.experimental import pallas as pl
from jax.experimental.pallas import tpu as pltpu
from jax.sharding import PartitionSpec as P

MESH = pl.DeviceIdType.MESH
ROWS = 16
KINDS = 'UDXMWFVZA'
PARTS = (2, 2, 2, 1, 1, 1, 1, 2)
EARLY = (1, 1, 0, 0, 1, 0, 1, 1, 1, 0, 1, 0)
SPLIT = (0, 0, 0, 0, 0, 0, 0, 0, 0, 1, 0, 0)
AHEAD = (1, 1, 0, 1, 1, 1, 1, 1, 1, 0, 1, 1)
ORDERS = (
    (
        33, 8080, 3, 8050, 13, 22, 43, 23, 2, 8030, 12, 8070, 8100, 63, 8010, 21, 1, 52, 8000, 11, 53, 8040,
        2000, 2010, 3000, 42, 2030, 51, 83, 3010, 41, 113, 62, 2040, 2020, 112, 32, 61, 103, 8060, 3040, 31,
        3020, 2060, 3030, 93, 4000, 3060, 8110, 73, 2050, 111, 2110, 4010, 2080, 72, 3050, 3110, 82, 102, 4040,
        92, 71, 81, 3080, 6040, 91, 101, 4060, 6010, 6000, 6030, 2090, 2070, 4090, 6020, 3070, 6050, 2100, 6090,
        3090, 6110, 3100, 4080, 6060, 4070, 4100, 6070, 7050, 6080, 7090, 7020, 7030, 6100, 7110,
    ),
    (
        8000, 8030, 8060, 8100, 33, 8110, 3, 8050, 13, 8080, 22, 43, 1030, 23, 1000, 2, 1010, 12, 1040, 8010,
        63, 2020, 3020, 1020, 2000, 52, 3000, 8040, 8070, 2010, 53, 1060, 5000, 5010, 5002, 42, 6020, 3010,
        1050, 2050, 5003, 83, 3050, 4000, 5013, 5012, 113, 2040, 5022, 62, 3040, 4010, 1080, 5040, 32, 1110,
        6050, 2060, 103, 5043, 5042, 112, 2030, 3030, 3060, 4040, 5060, 5052, 5062, 93, 73, 1100, 6030, 2110,
        5063, 3110, 1090, 5080, 4060, 72, 1070, 6040, 5032, 82, 92, 5083, 6000, 102, 2070, 3070, 2080, 6010,
        6110, 2090, 4090, 2100, 3090, 5072, 5082, 5070, 5112, 3080, 6090, 4080, 5100, 5050, 5020, 7090, 5073,
        5090, 6060, 3100, 5110, 4070, 5092, 5103, 5102, 4100, 5030, 5053, 5023, 6080, 5093, 5033, 5113, 6070,
        6100,
    ),
)


def moment_step(gradient, moment_one, moment_two):
    moment_one = 0.9 * moment_one + 0.1 * gradient
    moment_two = 0.95 * moment_two + 0.05 * gradient * gradient
    return moment_one, moment_two


def weight_step(moment_one, moment_two, weight):
    update = moment_one / (1.0 - 0.9**50) / (jnp.sqrt(moment_two / (1.0 - 0.95**50)) + 1e-08)
    return weight - 0.05 * (update + 0.1 * weight)


class Chunk(typing.NamedTuple):
    row: int
    col: int
    width: int
    early: bool
    split: bool
    ahead: bool


def job_list(dp, chunks, role):
    jobs = []
    for c, chunk in enumerate(chunks):
        jobs += [("U", c, k) for k in range(dp - 1, role, -1)] + [("D", c, k) for k in range(role)] + [("X", c, 0)]
        passed = [("F", c, k) for k in range(role - 1, -1, -1)]
        if role > 0:
            passed += [("F", c, k) for k in range(role + 1, dp)]
        if chunk.early:
            jobs += [("A", c, 0)] * chunk.ahead + [("M", c, 0)] + passed + [("W", c, 0), ("V", c, 0)]
        else:
            jobs += [("A", c, 0)] * chunk.ahead + [("W", c, 0)] * chunk.split + [("M", c, 0), ("V", c, 0)] + passed
            jobs += [("Z", c, 0)] * (chunk.split or role == 0)
    return jobs


def plan(dp, tile_rows, cols):
    tuned = (dp == len(ORDERS) * 2) and tile_rows == ROWS * len(PARTS) and cols % (128 * max(PARTS)) == 0
    parts = PARTS if tuned else (1,) * (tile_rows // ROWS)
    spans = [(i * ROWS, j * (cols // n), cols // n) for i, n in enumerate(parts) for j in range(n)]
    chunks = [
        Chunk(*span, *((EARLY[c] == 1, SPLIT[c] == 1, AHEAD[c] == 1) if tuned else (c % 2 == 0, False, False)))
        for c, span in enumerate(spans)
    ]
    orders = [job_list(dp, chunks, role) for role in range(dp // 2)]
    if tuned:
        orders = [
            [(KINDS[code // 1000], code // 10 % 100, code % 10) for code in coded] for coded in ORDERS
        ]
    return chunks, orders


def kernel(dp, peers, owners, chunks, orders, old_ref, new_ref, g_hbm, m_hbm, v_hbm, w_hbm, *rest):
    moments, params, rest = rest[0], rest[1], rest[2:]
    g, state, part, line = rest[:4]
    rest = rest[4:]
    count = len(chunks)
    fresh, mail, inbox, wide, wide_mail, wide_inbox, old_mail, old_inbox = (
        rest[i * count : (i + 1) * count] for i in range(8)
    )
    g_sem, in_sem, sent, z_recv, x_recv, w_recv, o_recv = rest[8 * count :]
    z = lax.axis_index("dp")
    e = lax.axis_index("expert")
    old_slots, cols = state.shape[1], state.shape[-1]
    new_slots = params.shape[0]
    far = jnp.where(z < dp // 2, 0, 1)
    place = jnp.where(z < dp // 2, z, dp - 1 - z)
    ahead = 1 - 2 * far
    owns = e < owners

    if peers & (peers - 1):
        targets = [lax.rem(e + step, peers) for step in range(peers)]
    else:
        bits = [1 << i for i in range(peers.bit_length() - 1)]
        turns = {bit: bit * (1 - 2 * lax.rem(e // bit, 2)) for bit in bits}
        targets = [e + sum(turns[bit] for bit in bits if mask & bit) for mask in (0, *range(peers - 1, 0, -1))]

    def rows(c):
        return pl.ds(chunks[c].row, ROWS)

    def span(c):
        return pl.ds(chunks[c].col, chunks[c].width)

    def real(k):
        return k + far * (dp - 1 - 2 * k)

    def block(c, k):
        return pl.ds(pl.multiple_of(real(k) * cols + chunks[c].col, 128), chunks[c].width)

    def wide_block(c, k, plane):
        return pl.ds(pl.multiple_of(lax.rem(k - plane + dp, dp) * chunks[c].width, 128), chunks[c].width)

    def mine(c):
        return pl.ds(pl.multiple_of(z * cols + chunks[c].col, 128), chunks[c].width)

    def way(right):
        return far if right else 1 - far

    def beside(right):
        return {"dp": z + ahead if right else z - ahead}

    g_loads = [
        pltpu.make_async_copy(g_hbm.at[0, :, pl.ds(row, ROWS)], g.at[:, pl.ds(row, ROWS)], g_sem.at[row // ROWS])
        for row in range(0, g.shape[1], ROWS)
    ]
    loads = [pltpu.make_async_copy(ref, state.at[i], in_sem) for i, ref in enumerate((m_hbm, v_hbm, w_hbm))]

    @pl.when(owns)
    def _():
        g_loads[0].start()

    barrier = pltpu.get_barrier_semaphore()
    for to in targets[1:]:
        pl.semaphore_signal(barrier, inc=1, device_id={"expert": to}, device_id_type=MESH)
    for step in (-1, 1):
        @pl.when((z + step >= 0) & (z + step < dp))
        def _():
            pl.semaphore_signal(barrier, inc=1, device_id={"dp": z + step}, device_id_type=MESH)

    @pl.when(owns)
    def _():
        for load in loads + g_loads[1:]:
            load.start()

    inner = (z > 0).astype(jnp.int32) + (z < dp - 1).astype(jnp.int32)
    pl.semaphore_wait(barrier, peers - 1 + inner)

    def route(tile, carry):
        sent, taken, slots, sources = carry
        old, new = old_ref[tile], new_ref[tile]
        leaves, comes = old == e, new == e
        slots = tuple(jnp.where(leaves & (new == to), sent, slot) for to, slot in zip(targets, slots))
        sources = tuple(
            jnp.where(comes & (taken == slot), old, source) for slot, source in enumerate(sources)
        )
        return sent + leaves.astype(jnp.int32), taken + comes.astype(jnp.int32), slots, sources

    def taken_by(sem, ref):
        pltpu.make_async_copy(ref, ref, sem).wait()

    def sum_copy(c, k, right, raw=False):
        src = g.at[:, rows(c), block(c, k)] if raw else part.at[real(k), :, rows(c), span(c)]
        return pltpu.make_async_remote_copy(
            src, line.at[way(right), real(k), :, rows(c), span(c)], sent, z_recv.at[c, real(k)],
            device_id=beside(right), device_id_type=MESH,
        )

    def gather_copy(c, k, right, to_end):
        src = dst = params.at[:, rows(c), block(c, k)]
        if chunks[c].early:
            src = wide[c].at[:, :, wide_block(c, real(k), z)]
            dst = wide[c].at[:, :, wide_block(c, real(k), beside(right)["dp"])]
        return pltpu.make_async_remote_copy(
            src, dst, sent, z_recv.at[c, real(1 if to_end else k)],
            device_id=beside(right), device_id_type=MESH,
        )

    def gather_send(c, k, right, role):
        gather_copy(c, k, right, role == 1 and not right).start()

    def gather_bytes(c, pieces):
        ref = g if chunks[c].early else params
        return ref.at[:, pl.ds(0, pieces * ROWS), pl.ds(0, chunks[c].width)]

    def mail_copy(c, to):
        return pltpu.make_async_remote_copy(
            mail[c].at[to], inbox[c].at[e], sent, x_recv.at[c],
            device_id={"expert": to}, device_id_type=MESH,
        )

    def mail_bytes(c, boxes):
        return mail[c].at[pl.ds(0, boxes)]

    def weights_copy(c, to):
        return pltpu.make_async_remote_copy(
            wide_mail[c].at[to], wide_inbox[c].at[e], sent, w_recv.at[c],
            device_id={"expert": to}, device_id_type=MESH,
        )

    def old_copy(c, to):
        return pltpu.make_async_remote_copy(
            old_mail[c].at[to], old_inbox[c].at[e], sent, o_recv.at[c],
            device_id={"expert": to}, device_id_type=MESH,
        )

    def weights_bytes(c, boxes):
        return wide_mail[c].at[pl.ds(0, boxes)]

    def arrived(c, k, right):
        return line[way(right), real(k), :, rows(c), span(c)].astype(jnp.float32)

    def add_and_send(c, k, right):
        sum_copy(c, k, right).wait_recv()
        total = g[:, rows(c), block(c, k)].astype(jnp.float32) + arrived(c, k, right)
        part[real(k), :, rows(c), span(c)] = total.astype(jnp.bfloat16)
        sum_copy(c, k, right).start()

    def gather(c, role):
        gather_send(c, role, True, role)
        if role > 0:
            gather_send(c, role, False, role)

    def update(c, role):
        sides = [right for right in (True, False) if role > 0 or not right]
        at = line.at[pl.ds(0, len(sides)), z, :, rows(c), span(c)]
        taken_by(z_recv.at[c, z], at)
        for slot in range(old_slots):
            gradient = g[slot, rows(c), mine(c)].astype(jnp.float32)
            for right in sides:
                gradient += line[way(right), z, slot, rows(c), span(c)].astype(jnp.float32)
            values = list(moment_step(gradient, *(state[i, slot, rows(c), span(c)] for i in range(2))))
            if chunks[c].early or not chunks[c].ahead:
                values.insert(0, weight_step(*values, state[2, slot, rows(c), span(c)]))
            values = [value.astype(jnp.bfloat16) for value in values]
            if chunks[c].early:
                wide[c][slot, :, pl.ds(0, chunks[c].width)] = values.pop(0)
            elif chunks[c].split:
                wide[c][slot] = values.pop(0)
            for i, value in enumerate(values):
                fresh[c][slot, i] = value
        if chunks[c].early:
            gather(c, role)

    def post(c, slots):
        for to, slot in zip(targets[1:], slots[1:]):
            mail[c][to] = fresh[c][slot]
            mail_copy(c, to).start()
        inbox[c][e] = fresh[c][slots[0]]

    def last_arrivals(c, role):
        if role == 0:
            taken_by(z_recv.at[c, real(1)], gather_bytes(c, dp - 1))

    def post_old_weights(c, slots):
        for to, slot in zip(targets[1:], slots[1:]):
            old_mail[c][to] = state[2, slot, rows(c), span(c)].astype(jnp.bfloat16)
            old_copy(c, to).start()
        old_inbox[c][e] = state[2, slots[0], rows(c), span(c)].astype(jnp.bfloat16)

    def post_weights(c, role, slots):
        if chunks[c].early:
            last_arrivals(c, role)
        size = wide_mail[c].shape[2]
        columns = pl.ds(wide[c].shape[2] - size, size)
        for to, slot in zip(targets[1:], slots[1:]):
            wide_mail[c][to] = wide[c][slot, :, columns]
            weights_copy(c, to).start()
        wide_inbox[c][e] = wide[c][slots[0], :, columns]

    def receive(c, moments_too, weights_too, old_too):
        for mask, boxes in ((owns, owners - 1), (e >= owners, owners)):
            @pl.when(mask)
            def _():
                if moments_too:
                    taken_by(x_recv.at[c], mail_bytes(c, boxes))
                if weights_too:
                    taken_by(w_recv.at[c], weights_bytes(c, boxes))
                if old_too:
                    taken_by(o_recv.at[c], old_mail[c].at[pl.ds(0, boxes)])

    def kept(slot, taken, value):
        return jnp.where(taken > slot, value, jnp.zeros_like(value))

    def place_moments(c, taken, sources):
        first = inbox[c].shape[1] - 2
        for slot in range(new_slots):
            for i in range(2):
                moments[i, slot, rows(c), span(c)] = kept(slot, taken, inbox[c][sources[slot], first + i])

    def deliver(c, role, taken, sources):
        width = chunks[c].width
        receive(c, not chunks[c].split, chunks[c].early or chunks[c].split, chunks[c].ahead)
        for slot in range(new_slots):
            if chunks[c].ahead:
                values = [inbox[c][sources[slot], i] for i in range(2)] + [old_inbox[c][sources[slot]]]
                own = weight_step(*(value.astype(jnp.float32) for value in values)).astype(jnp.bfloat16)
            elif chunks[c].early:
                own = wide_inbox[c][sources[slot], :, pl.ds(0, width)]
            else:
                own = wide_inbox[c][sources[slot]] if chunks[c].split else inbox[c][sources[slot], 0]
            params[slot, rows(c), mine(c)] = kept(slot, taken, own)
            for step in range(1, dp if chunks[c].early else 1):
                column = pl.multiple_of(lax.rem(z + step, dp) * cols + chunks[c].col, 128)
                first = (step - 1 if chunks[c].ahead else step) * width
                value = wide_inbox[c][sources[slot], :, pl.ds(first, width)]
                params[slot, rows(c), pl.ds(column, width)] = kept(slot, taken, value)
        if not chunks[c].early:
            gather(c, role)
        if not chunks[c].split:
            place_moments(c, taken, sources)

    def finish(c, role, taken, sources):
        if chunks[c].split:
            receive(c, True, False, False)
            place_moments(c, taken, sources)
        last_arrivals(c, role)

    def run(role, order, slots, taken, sources, loaded):
        for kind, c, k in order:
            by_owners = kind in "UDXMWA" or (kind == "F" and chunks[c].early)

            def job():
                if kind in "UDX" and chunks[c].row not in loaded:
                    loaded.append(chunks[c].row)
                    g_loads[chunks[c].row // ROWS].wait()
                if kind in "XA" and -1 not in loaded:
                    loaded.append(-1)
                    taken_by(in_sem, state)
                if kind == "U" and role == 0:
                    sum_copy(c, k, True, True).start()
                elif kind in "UD":
                    add_and_send(c, k, kind == "U")
                elif kind == "X":
                    update(c, role)
                elif kind == "A":
                    post_old_weights(c, slots)
                elif kind == "M":
                    post(c, slots)
                elif kind == "F":
                    gather_copy(c, k, k < role, False).wait_recv()
                    gather_send(c, k, k < role, role)
                elif kind == "W":
                    post_weights(c, role, slots)
                elif kind == "V":
                    deliver(c, role, taken, sources)
                else:
                    finish(c, role, taken, sources)

            if by_owners:
                pl.when(owns)(job)
            else:
                job()

    lead = 0
    while orders[0][lead][:2] == ("U", 0):
        lead += 1
    loaded = [[] for _ in orders]

    @pl.when(place == 0)
    def _():
        run(0, orders[0][:lead], None, None, None, loaded[0])

    zero = jnp.int32(0)
    _, taken, slots, sources = lax.fori_loop(
        0, old_ref.shape[0], route, (zero, zero, (zero,) * peers, (zero,) * new_slots)
    )
    slots = tuple(jnp.minimum(slot, old_slots - 1) for slot in slots)
    sources = tuple(jnp.minimum(source, owners - 1) for source in sources)

    for role, order in enumerate(orders):
        @pl.when(place == role)
        def _():
            run(role, order[lead:] if role == 0 else order, slots, taken, sources, loaded[role])

            def gathers_sent(c):
                taken_by(sent, gather_bytes(c, dp + 1 if role > 0 else 1))

            for c in range(count):
                if not chunks[c].early:
                    gathers_sent(c)

            @pl.when(owns)
            def _():
                for c in range(count):
                    if chunks[c].early:
                        gathers_sent(c)

    @pl.when(owns)
    def _():
        taken_by(sent, part.at[pl.ds(0, dp - 1)])
        for c in range(count):
            taken_by(sent, mail_bytes(c, peers - 1))
            if chunks[c].early or chunks[c].split:
                taken_by(sent, weights_bytes(c, peers - 1))
            if chunks[c].ahead:
                taken_by(sent, old_mail[c].at[pl.ds(0, peers - 1)])


def widen(moments, params, w_out, m_out, v_out, p_out, staged, sems):
    new_slots, _, cols = w_out.shape
    z = lax.axis_index("dp")
    mine = pl.ds(pl.multiple_of(z * cols, cols), cols)
    pltpu.make_async_copy(params, p_out, sems.at[3]).start()
    for slot in range(new_slots):
        parts = (params.at[slot, :, mine], moments.at[0, slot], moments.at[1, slot])
        for i, (part, out) in enumerate(zip(parts, (w_out, m_out, v_out))):
            staged[i, slot] = part[...].astype(jnp.float32)
            pltpu.make_async_copy(staged.at[i, slot], out.at[slot], sems.at[i]).start()
    for i, out in enumerate((w_out, m_out, v_out, p_out)):
        pltpu.make_async_copy(out, out, sems.at[i]).wait()


def shards(grad_parts, first_moment, second_moment, master_weight, old_owner, new_owner):
    dp = lax.axis_size("dp")
    peers = lax.axis_size("expert")
    old_slots, tile_rows, cols = first_moment.shape
    owners = old_owner.shape[0] // old_slots
    new_slots = min(old_slots + old_slots // 2, peers - peers // 5)
    chunks, orders = plan(dp, tile_rows, cols)
    count = len(chunks)
    bf16, f32 = jnp.bfloat16, jnp.float32
    dma = pltpu.SemaphoreType.DMA
    any_space = pl.BlockSpec(memory_space=pl.ANY)
    smem = pl.BlockSpec(memory_space=pltpu.SMEM)
    vmem = pl.BlockSpec(memory_space=pltpu.VMEM)
    master = jax.ShapeDtypeStruct((new_slots, tile_rows, cols), f32)
    scratch = [
        pltpu.VMEM((old_slots, tile_rows, dp * cols), bf16),
        pltpu.VMEM((3, old_slots, tile_rows, cols), f32),
        pltpu.VMEM((dp, old_slots, tile_rows, cols), bf16),
        pltpu.VMEM((2, dp, old_slots, tile_rows, cols), bf16),
    ]
    kept = [2 if chunk.early or chunk.split or chunk.ahead else 3 for chunk in chunks]
    wide = [chunk.width * (dp if chunk.early else 1) if chunk.early or chunk.split else 128 for chunk in chunks]
    sent = [size - chunk.width if chunk.early and chunk.ahead else size for size, chunk in zip(wide, chunks)]
    old = [chunk.width if chunk.ahead else 128 for chunk in chunks]
    for boxes in (old_slots, peers, owners):
        scratch += [pltpu.VMEM((boxes, n, ROWS, chunk.width), bf16) for n, chunk in zip(kept, chunks)]
    for boxes, sizes in ((old_slots, wide), (peers, sent), (owners, sent), (peers, old), (owners, old)):
        scratch += [pltpu.VMEM((boxes, ROWS, n), bf16) for n in sizes]
    scratch += [dma((tile_rows // ROWS,)), dma, dma, dma((count, dp))]
    scratch += [dma((count,))] * 3
    results = new_slots * tile_rows * cols * (4 + 2 * dp)
    moments, params = pl.pallas_call(
        functools.partial(kernel, dp, peers, owners, chunks, orders),
        out_shape=(
            pltpu.VMEM((2, new_slots, tile_rows, cols), bf16),
            pltpu.VMEM((new_slots, tile_rows, dp * cols), bf16),
        ),
        in_specs=[smem] * 2 + [any_space] * 4,
        out_specs=(vmem,) * 2,
        scratch_shapes=scratch,
        compiler_params=pltpu.CompilerParams(
            collective_id=0, has_side_effects=True, vmem_limit_bytes=67043328 - results - 2**19
        ),
    )(old_owner, new_owner, grad_parts, first_moment, second_moment, master_weight)
    return pl.pallas_call(
        widen,
        out_shape=(master,) * 3
        + (jax.ShapeDtypeStruct((new_slots, tile_rows, dp * cols), bf16),),
        in_specs=[vmem] * 2,
        out_specs=(any_space,) * 4,
        scratch_shapes=[pltpu.VMEM((3, new_slots, tile_rows, cols), f32), dma((4,))],
        compiler_params=pltpu.CompilerParams(vmem_limit_bytes=2**24),
    )(moments, params)


def solution(mesh):
    placed = (
        P("dp", "expert", None, None),
        P("expert", None, "dp"),
        P("expert", None, "dp"),
        P("expert", None, "dp"),
        P(),
        P(),
    )
    return jax.shard_map(
        shards,
        mesh=mesh,
        in_specs=placed,
        out_specs=(
            P("expert", None, "dp"),
            P("expert", None, "dp"),
            P("expert", None, "dp"),
            P("expert", None, None),
        ),
        check_vma=False,
    )
```

```python
import functools
import typing

import jax
import jax.numpy as jnp
from jax import lax
from jax.experimental import pallas as pl
from jax.experimental.pallas import tpu as pltpu
from jax.sharding import PartitionSpec as P

MESH = pl.DeviceIdType.MESH
ROWS = 16
KINDS = 'UDXMWFVZA'
PARTS = (2, 2, 2, 1, 1, 1, 1, 2)
EARLY = (1, 1, 0, 0, 1, 0, 1, 1, 1, 0, 1, 0)
SPLIT = (0, 0, 0, 1, 0, 0, 0, 0, 0, 1, 0, 0)
AHEAD = (1, 1, 0, 0, 1, 1, 1, 1, 1, 0, 1, 1)
ORDERS = (
    (
        33, 13, 3, 53, 22, 8070, 23, 8080, 8100, 2, 63, 12, 8060, 21, 43, 1, 52, 8110, 8010, 8000, 2030, 8040,
        2010, 11, 2000, 3010, 51, 42, 32, 83, 62, 8050, 41, 103, 113, 61, 2050, 2020, 3020, 3050, 31, 3030,
        3000, 2040, 2060, 3040, 4000, 4010, 73, 93, 4030, 72, 112, 3060, 71, 82, 2080, 111, 81, 3080, 102, 6000,
        2110, 4040, 92, 6030, 4060, 2100, 101, 3110, 2090, 6040, 2070, 91, 4090, 3070, 6020, 6050, 6110, 3100,
        4080, 6090, 6060, 4100, 4070, 7020, 6080, 3090, 6100, 6010, 7110, 6070, 7050, 7030, 7090,
    ),
    (
        8080, 8110, 8000, 8060, 8050, 8070, 33, 13, 8010, 3, 53, 8040, 22, 1030, 23, 1010, 2, 1000, 63, 12,
        1050, 2020, 3020, 1020, 43, 2000, 52, 1060, 5010, 3000, 2010, 5000, 1040, 6020, 2050, 3050, 5002, 8100,
        42, 5012, 5013, 4010, 32, 5003, 83, 3010, 5022, 4000, 62, 6050, 2040, 113, 3040, 1080, 103, 2060, 2030,
        4030, 5052, 3030, 5040, 5042, 3060, 5060, 1110, 73, 1100, 5062, 5043, 4040, 93, 5063, 72, 1070, 6030,
        112, 4060, 82, 1090, 2070, 2110, 7030, 3110, 5032, 5080, 3070, 2080, 102, 3080, 6000, 92, 5072, 5030,
        6040, 5083, 5100, 5082, 2100, 5070, 3100, 6110, 2090, 4090, 6010, 5033, 5103, 5020, 6060, 5102, 4100,
        5073, 5110, 4080, 4070, 6090, 5113, 6100, 5050, 5090, 3090, 5023, 5092, 5112, 5053, 6080, 5093, 6070,
        7090,
    ),
)


def moment_step(gradient, moment_one, moment_two):
    moment_one = 0.9 * moment_one + 0.1 * gradient
    moment_two = 0.95 * moment_two + 0.05 * gradient * gradient
    return moment_one, moment_two


def weight_step(moment_one, moment_two, weight):
    update = moment_one / (1.0 - 0.9**50) / (jnp.sqrt(moment_two / (1.0 - 0.95**50)) + 1e-08)
    return weight - 0.05 * (update + 0.1 * weight)


class Chunk(typing.NamedTuple):
    row: int
    col: int
    width: int
    early: bool
    split: bool
    ahead: bool


def job_list(dp, chunks, role):
    jobs = []
    for c, chunk in enumerate(chunks):
        jobs += [("U", c, k) for k in range(dp - 1, role, -1)] + [("D", c, k) for k in range(role)] + [("X", c, 0)]
        passed = [("F", c, k) for k in range(role - 1, -1, -1)]
        if role > 0:
            passed += [("F", c, k) for k in range(role + 1, dp)]
        if chunk.early:
            jobs += [("A", c, 0)] * chunk.ahead + [("M", c, 0)] + passed + [("W", c, 0), ("V", c, 0)]
        else:
            jobs += [("A", c, 0)] * chunk.ahead + [("W", c, 0)] * chunk.split + [("M", c, 0), ("V", c, 0)] + passed
            jobs += [("Z", c, 0)] * (chunk.split or role == 0)
    return jobs


def plan(dp, tile_rows, cols):
    tuned = (dp == len(ORDERS) * 2) and tile_rows == ROWS * len(PARTS) and cols % (128 * max(PARTS)) == 0
    parts = PARTS if tuned else (1,) * (tile_rows // ROWS)
    spans = [(i * ROWS, j * (cols // n), cols // n) for i, n in enumerate(parts) for j in range(n)]
    chunks = [
        Chunk(*span, *((EARLY[c] == 1, SPLIT[c] == 1, AHEAD[c] == 1) if tuned else (c % 2 == 0, False, False)))
        for c, span in enumerate(spans)
    ]
    orders = [job_list(dp, chunks, role) for role in range(dp // 2)]
    if tuned:
        orders = [
            [(KINDS[code // 1000], code // 10 % 100, code % 10) for code in coded] for coded in ORDERS
        ]
    start = [job[0] == "X" for job in orders[0]].index(True)
    orders[0][:start] = sorted(orders[0][:start], key=lambda job: job[0] != "U")
    return chunks, orders


def kernel(dp, peers, owners, chunks, orders, old_ref, new_ref, g_hbm, m_hbm, v_hbm, w_hbm, *rest):
    moments, params, rest = rest[0], rest[1], rest[2:]
    g, state, weights, part, line = rest[:5]
    rest = rest[5:]
    count = len(chunks)
    fresh, mail, inbox, wide, wide_mail, wide_inbox, old_mail, old_inbox = (
        rest[i * count : (i + 1) * count] for i in range(8)
    )
    g_sem, old_sem, in_sem, sent, z_recv, x_recv, w_recv, o_recv = rest[8 * count :]
    z = lax.axis_index("dp")
    e = lax.axis_index("expert")
    old_slots, cols = state.shape[1], state.shape[-1]
    new_slots = params.shape[0]
    far = jnp.where(z < dp // 2, 0, 1)
    place = jnp.where(z < dp // 2, z, dp - 1 - z)
    ahead = 1 - 2 * far
    owns = e < owners

    if peers & (peers - 1):
        targets = [lax.rem(e + step, peers) for step in range(peers)]
    else:
        bits = [1 << i for i in range(peers.bit_length() - 1)]
        turns = {bit: bit * (1 - 2 * lax.rem(e // bit, 2)) for bit in bits}
        targets = [e + sum(turns[bit] for bit in bits if mask & bit) for mask in (0, *range(peers - 1, 0, -1))]

    def rows(c):
        return pl.ds(chunks[c].row, ROWS)

    def span(c):
        return pl.ds(chunks[c].col, chunks[c].width)

    def real(k):
        return k + far * (dp - 1 - 2 * k)

    def block(c, k):
        return pl.ds(pl.multiple_of(real(k) * cols + chunks[c].col, 128), chunks[c].width)

    def wide_block(c, k, plane):
        return pl.ds(pl.multiple_of(lax.rem(k - plane + dp, dp) * chunks[c].width, 128), chunks[c].width)

    def mine(c):
        return pl.ds(pl.multiple_of(z * cols + chunks[c].col, 128), chunks[c].width)

    def way(right):
        return far if right else 1 - far

    def beside(right):
        return {"dp": z + ahead if right else z - ahead}

    g_loads = [
        pltpu.make_async_copy(g_hbm.at[0, :, pl.ds(row, ROWS)], g.at[:, pl.ds(row, ROWS)], g_sem.at[row // ROWS])
        for row in range(0, g.shape[1], ROWS)
    ]
    loads = [pltpu.make_async_copy(w_hbm, weights, old_sem)]
    loads += [pltpu.make_async_copy(ref, state.at[i], in_sem) for i, ref in enumerate((m_hbm, v_hbm))]

    @pl.when(owns)
    def _():
        g_loads[0].start()

    barrier = pltpu.get_barrier_semaphore()
    for to in targets[1:]:
        pl.semaphore_signal(barrier, inc=1, device_id={"expert": to}, device_id_type=MESH)
    for step in (-1, 1):
        @pl.when((z + step >= 0) & (z + step < dp))
        def _():
            pl.semaphore_signal(barrier, inc=1, device_id={"dp": z + step}, device_id_type=MESH)

    @pl.when(owns)
    def _():
        for load in g_loads[1:3] + loads[:1] + g_loads[3:] + loads[1:]:
            load.start()

    inner = (z > 0).astype(jnp.int32) + (z < dp - 1).astype(jnp.int32)
    pl.semaphore_wait(barrier, peers - 1 + inner)

    def route(tile, carry):
        sent, taken, slots, sources = carry
        old, new = old_ref[tile], new_ref[tile]
        leaves, comes = old == e, new == e
        slots = tuple(jnp.where(leaves & (new == to), sent, slot) for to, slot in zip(targets, slots))
        sources = tuple(
            jnp.where(comes & (taken == slot), old, source) for slot, source in enumerate(sources)
        )
        return sent + leaves.astype(jnp.int32), taken + comes.astype(jnp.int32), slots, sources

    def taken_by(sem, ref):
        pltpu.make_async_copy(ref, ref, sem).wait()

    def sum_copy(c, k, right, raw=False):
        src = g.at[:, rows(c), block(c, k)] if raw else part.at[real(k), :, rows(c), span(c)]
        return pltpu.make_async_remote_copy(
            src, line.at[way(right), real(k), :, rows(c), span(c)], sent, z_recv.at[c, real(k)],
            device_id=beside(right), device_id_type=MESH,
        )

    def gather_copy(c, k, right, to_end):
        src = dst = params.at[:, rows(c), block(c, k)]
        if chunks[c].early:
            src = wide[c].at[:, :, wide_block(c, real(k), z)]
            dst = wide[c].at[:, :, wide_block(c, real(k), beside(right)["dp"])]
        return pltpu.make_async_remote_copy(
            src, dst, sent, z_recv.at[c, real(1 if to_end else k)],
            device_id=beside(right), device_id_type=MESH,
        )

    def gather_send(c, k, right, role):
        gather_copy(c, k, right, role == 1 and not right).start()

    def gather_bytes(c, pieces):
        ref = g if chunks[c].early else params
        return ref.at[:, pl.ds(0, pieces * ROWS), pl.ds(0, chunks[c].width)]

    def mail_copy(c, to):
        return pltpu.make_async_remote_copy(
            mail[c].at[to], inbox[c].at[e], sent, x_recv.at[c],
            device_id={"expert": to}, device_id_type=MESH,
        )

    def mail_bytes(c, boxes):
        return mail[c].at[pl.ds(0, boxes)]

    def weights_copy(c, to):
        return pltpu.make_async_remote_copy(
            wide_mail[c].at[to], wide_inbox[c].at[e], sent, w_recv.at[c],
            device_id={"expert": to}, device_id_type=MESH,
        )

    def old_copy(c, to):
        return pltpu.make_async_remote_copy(
            old_mail[c].at[to], old_inbox[c].at[e], sent, o_recv.at[c],
            device_id={"expert": to}, device_id_type=MESH,
        )

    def weights_bytes(c, boxes):
        return wide_mail[c].at[pl.ds(0, boxes)]

    def arrived(c, k, right):
        return line[way(right), real(k), :, rows(c), span(c)].astype(jnp.float32)

    def add_and_send(c, k, right):
        sum_copy(c, k, right).wait_recv()
        total = g[:, rows(c), block(c, k)].astype(jnp.float32) + arrived(c, k, right)
        part[real(k), :, rows(c), span(c)] = total.astype(jnp.bfloat16)
        sum_copy(c, k, right).start()

    def gather(c, role):
        gather_send(c, role, True, role)
        if role > 0:
            gather_send(c, role, False, role)

    def update(c, role):
        sides = [right for right in (True, False) if role > 0 or not right]
        at = line.at[pl.ds(0, len(sides)), z, :, rows(c), span(c)]
        taken_by(z_recv.at[c, z], at)
        for slot in range(old_slots):
            gradient = g[slot, rows(c), mine(c)].astype(jnp.float32)
            for right in sides:
                gradient += line[way(right), z, slot, rows(c), span(c)].astype(jnp.float32)
            values = list(moment_step(gradient, *(state[i, slot, rows(c), span(c)] for i in range(2))))
            if chunks[c].early or not chunks[c].ahead:
                values.insert(0, weight_step(*values, weights[slot, rows(c), span(c)]))
            values = [value.astype(jnp.bfloat16) for value in values]
            if chunks[c].early:
                wide[c][slot, :, pl.ds(0, chunks[c].width)] = values.pop(0)
            elif chunks[c].split:
                wide[c][slot] = values.pop(0)
            for i, value in enumerate(values):
                fresh[c][slot, i] = value
        if chunks[c].early:
            gather(c, role)

    def post(c, slots):
        for to, slot in zip(targets[1:], slots[1:]):
            mail[c][to] = fresh[c][slot]
            mail_copy(c, to).start()
        inbox[c][e] = fresh[c][slots[0]]

    def last_arrivals(c, role):
        if role == 0:
            taken_by(z_recv.at[c, real(1)], gather_bytes(c, dp - 1))

    def post_old_weights(c, slots):
        for to, slot in zip(targets[1:], slots[1:]):
            old_mail[c][to] = weights[slot, rows(c), span(c)].astype(jnp.bfloat16)
            old_copy(c, to).start()
        old_inbox[c][e] = weights[slots[0], rows(c), span(c)].astype(jnp.bfloat16)

    def post_weights(c, role, slots):
        if chunks[c].early:
            last_arrivals(c, role)
        size = wide_mail[c].shape[2]
        columns = pl.ds(wide[c].shape[2] - size, size)
        for to, slot in zip(targets[1:], slots[1:]):
            wide_mail[c][to] = wide[c][slot, :, columns]
            weights_copy(c, to).start()
        wide_inbox[c][e] = wide[c][slots[0], :, columns]

    def receive(c, moments_too, weights_too, old_too):
        for mask, boxes in ((owns, owners - 1), (e >= owners, owners)):
            @pl.when(mask)
            def _():
                if moments_too:
                    taken_by(x_recv.at[c], mail_bytes(c, boxes))
                if weights_too:
                    taken_by(w_recv.at[c], weights_bytes(c, boxes))
                if old_too:
                    taken_by(o_recv.at[c], old_mail[c].at[pl.ds(0, boxes)])

    def kept(slot, taken, value):
        return jnp.where(taken > slot, value, jnp.zeros_like(value))

    def place_moments(c, taken, sources):
        first = inbox[c].shape[1] - 2
        for slot in range(new_slots):
            for i in range(2):
                moments[i, slot, rows(c), span(c)] = kept(slot, taken, inbox[c][sources[slot], first + i])

    def deliver(c, role, taken, sources):
        width = chunks[c].width
        receive(c, not chunks[c].split, chunks[c].early or chunks[c].split, chunks[c].ahead)
        for slot in range(new_slots):
            if chunks[c].ahead:
                values = [inbox[c][sources[slot], i] for i in range(2)] + [old_inbox[c][sources[slot]]]
                own = weight_step(*(value.astype(jnp.float32) for value in values)).astype(jnp.bfloat16)
            elif chunks[c].early:
                own = wide_inbox[c][sources[slot], :, pl.ds(0, width)]
            else:
                own = wide_inbox[c][sources[slot]] if chunks[c].split else inbox[c][sources[slot], 0]
            params[slot, rows(c), mine(c)] = kept(slot, taken, own)
            for step in range(1, dp if chunks[c].early else 1):
                column = pl.multiple_of(lax.rem(z + step, dp) * cols + chunks[c].col, 128)
                first = (step - 1 if chunks[c].ahead else step) * width
                value = wide_inbox[c][sources[slot], :, pl.ds(first, width)]
                params[slot, rows(c), pl.ds(column, width)] = kept(slot, taken, value)
        if not chunks[c].early:
            gather(c, role)
        if not chunks[c].split:
            place_moments(c, taken, sources)

    def finish(c, role, taken, sources):
        if chunks[c].split:
            receive(c, True, False, False)
            place_moments(c, taken, sources)
        last_arrivals(c, role)

    def run(role, order, slots, taken, sources, loaded):
        for kind, c, k in order:
            by_owners = kind in "UDXMWA" or (kind == "F" and chunks[c].early)

            def job():
                if kind in "UDX" and chunks[c].row not in loaded:
                    loaded.append(chunks[c].row)
                    g_loads[chunks[c].row // ROWS].wait()
                if kind in "XA" and -1 not in loaded:
                    loaded.append(-1)
                    loads[0].wait()
                if kind == "X" and -2 not in loaded:
                    loaded.append(-2)
                    taken_by(in_sem, state)
                if kind == "U" and role == 0:
                    sum_copy(c, k, True, True).start()
                elif kind in "UD":
                    add_and_send(c, k, kind == "U")
                elif kind == "X":
                    update(c, role)
                elif kind == "A":
                    post_old_weights(c, slots)
                elif kind == "M":
                    post(c, slots)
                elif kind == "F":
                    gather_copy(c, k, k < role, False).wait_recv()
                    gather_send(c, k, k < role, role)
                elif kind == "W":
                    post_weights(c, role, slots)
                elif kind == "V":
                    deliver(c, role, taken, sources)
                else:
                    finish(c, role, taken, sources)

            if by_owners:
                pl.when(owns)(job)
            else:
                job()

    lead = 0
    while orders[0][lead][0] == "U":
        lead += 1
    loaded = [[] for _ in orders]

    @pl.when(place == 0)
    def _():
        run(0, orders[0][:lead], None, None, None, loaded[0])

    zero = jnp.int32(0)
    _, taken, slots, sources = lax.fori_loop(
        0, old_ref.shape[0], route, (zero, zero, (zero,) * peers, (zero,) * new_slots)
    )
    slots = tuple(jnp.minimum(slot, old_slots - 1) for slot in slots)
    sources = tuple(jnp.minimum(source, owners - 1) for source in sources)

    for role, order in enumerate(orders):
        @pl.when(place == role)
        def _():
            run(role, order[lead:] if role == 0 else order, slots, taken, sources, loaded[role])

            def gathers_sent(c):
                taken_by(sent, gather_bytes(c, dp + 1 if role > 0 else 1))

            for c in range(count):
                if not chunks[c].early:
                    gathers_sent(c)

            @pl.when(owns)
            def _():
                for c in range(count):
                    if chunks[c].early:
                        gathers_sent(c)

    @pl.when(owns)
    def _():
        taken_by(sent, part.at[pl.ds(0, dp - 1)])
        for c in range(count):
            taken_by(sent, mail_bytes(c, peers - 1))
            if chunks[c].early or chunks[c].split:
                taken_by(sent, weights_bytes(c, peers - 1))
            if chunks[c].ahead:
                taken_by(sent, old_mail[c].at[pl.ds(0, peers - 1)])


def widen(moments, params, w_out, m_out, v_out, p_out, staged, sems):
    new_slots, _, cols = w_out.shape
    z = lax.axis_index("dp")
    mine = pl.ds(pl.multiple_of(z * cols, cols), cols)
    pltpu.make_async_copy(params, p_out, sems.at[3]).start()
    for slot in range(new_slots):
        parts = (params.at[slot, :, mine], moments.at[0, slot], moments.at[1, slot])
        for i, (part, out) in enumerate(zip(parts, (w_out, m_out, v_out))):
            staged[i, slot] = part[...].astype(jnp.float32)
            pltpu.make_async_copy(staged.at[i, slot], out.at[slot], sems.at[i]).start()
    for i, out in enumerate((w_out, m_out, v_out, p_out)):
        pltpu.make_async_copy(out, out, sems.at[i]).wait()


def shards(grad_parts, first_moment, second_moment, master_weight, old_owner, new_owner):
    dp = lax.axis_size("dp")
    peers = lax.axis_size("expert")
    old_slots, tile_rows, cols = first_moment.shape
    owners = old_owner.shape[0] // old_slots
    new_slots = min(old_slots + old_slots // 2, peers - peers // 5)
    chunks, orders = plan(dp, tile_rows, cols)
    count = len(chunks)
    bf16, f32 = jnp.bfloat16, jnp.float32
    dma = pltpu.SemaphoreType.DMA
    any_space = pl.BlockSpec(memory_space=pl.ANY)
    smem = pl.BlockSpec(memory_space=pltpu.SMEM)
    vmem = pl.BlockSpec(memory_space=pltpu.VMEM)
    master = jax.ShapeDtypeStruct((new_slots, tile_rows, cols), f32)
    scratch = [
        pltpu.VMEM((old_slots, tile_rows, dp * cols), bf16),
        pltpu.VMEM((2, old_slots, tile_rows, cols), f32),
        pltpu.VMEM((old_slots, tile_rows, cols), f32),
        pltpu.VMEM((dp, old_slots, tile_rows, cols), bf16),
        pltpu.VMEM((2, dp, old_slots, tile_rows, cols), bf16),
    ]
    kept = [2 if chunk.early or chunk.split or chunk.ahead else 3 for chunk in chunks]
    wide = [chunk.width * (dp if chunk.early else 1) if chunk.early or chunk.split else 128 for chunk in chunks]
    sent = [size - chunk.width if chunk.early and chunk.ahead else size for size, chunk in zip(wide, chunks)]
    old = [chunk.width if chunk.ahead else 128 for chunk in chunks]
    for boxes in (old_slots, peers, owners):
        scratch += [pltpu.VMEM((boxes, n, ROWS, chunk.width), bf16) for n, chunk in zip(kept, chunks)]
    for boxes, sizes in ((old_slots, wide), (peers, sent), (owners, sent), (peers, old), (owners, old)):
        scratch += [pltpu.VMEM((boxes, ROWS, n), bf16) for n in sizes]
    scratch += [dma((tile_rows // ROWS,)), dma, dma, dma, dma((count, dp))]
    scratch += [dma((count,))] * 3
    results = new_slots * tile_rows * cols * (4 + 2 * dp)
    moments, params = pl.pallas_call(
        functools.partial(kernel, dp, peers, owners, chunks, orders),
        out_shape=(
            pltpu.VMEM((2, new_slots, tile_rows, cols), bf16),
            pltpu.VMEM((new_slots, tile_rows, dp * cols), bf16),
        ),
        in_specs=[smem] * 2 + [any_space] * 4,
        out_specs=(vmem,) * 2,
        scratch_shapes=scratch,
        compiler_params=pltpu.CompilerParams(
            collective_id=0, has_side_effects=True, vmem_limit_bytes=67043328 - results - 2**19
        ),
    )(old_owner, new_owner, grad_parts, first_moment, second_moment, master_weight)
    return pl.pallas_call(
        widen,
        out_shape=(master,) * 3
        + (jax.ShapeDtypeStruct((new_slots, tile_rows, dp * cols), bf16),),
        in_specs=[vmem] * 2,
        out_specs=(any_space,) * 4,
        scratch_shapes=[pltpu.VMEM((3, new_slots, tile_rows, cols), f32), dma((4,))],
        compiler_params=pltpu.CompilerParams(vmem_limit_bytes=2**24),
    )(moments, params)


def solution(mesh):
    placed = (
        P("dp", "expert", None, None),
        P("expert", None, "dp"),
        P("expert", None, "dp"),
        P("expert", None, "dp"),
        P(),
        P(),
    )
    return jax.shard_map(
        shards,
        mesh=mesh,
        in_specs=placed,
        out_specs=(
            P("expert", None, "dp"),
            P("expert", None, "dp"),
            P("expert", None, "dp"),
            P("expert", None, None),
        ),
        check_vma=False,
    )
```

```python
import functools
import typing

import jax
import jax.numpy as jnp
from jax import lax
from jax.experimental import pallas as pl
from jax.experimental.pallas import tpu as pltpu
from jax.sharding import PartitionSpec as P

MESH = pl.DeviceIdType.MESH
ROWS = 16
KINDS = 'UDXMWFVZA'
PARTS = (2, 2, 2, 1, 1, 1, 1, 2)
EARLY = (1, 1, 0, 0, 1, 0, 1, 1, 1, 0, 1, 0)
SPLIT = (0, 0, 1, 0, 0, 0, 0, 0, 0, 1, 0, 0)
AHEAD = (1, 1, 0, 0, 1, 1, 1, 1, 1, 0, 1, 1)
ORDERS = (
    (
        3, 8080, 8060, 43, 13, 23, 8110, 22, 63, 33, 8000, 42, 8070, 2, 53, 12, 8040, 8050, 21, 41, 8100, 52, 1,
        11, 2040, 8010, 2010, 3010, 51, 83, 2000, 103, 2020, 3020, 62, 113, 2060, 32, 61, 31, 3000, 3060, 2030,
        93, 72, 112, 3030, 73, 4040, 2050, 82, 71, 3050, 4010, 111, 2080, 4000, 81, 3080, 4020, 102, 2100, 2110,
        3110, 92, 4060, 6020, 3040, 6050, 2090, 101, 6010, 6000, 4090, 3090, 2070, 91, 3070, 3100, 6060, 6110,
        6030, 6090, 6040, 4080, 4100, 4070, 7030, 7110, 7050, 6080, 6100, 7020, 6070, 7090,
    ),
    (
        3, 8110, 43, 8070, 13, 22, 1000, 8050, 8060, 23, 8100, 1040, 8000, 8010, 63, 1010, 8080, 33, 42, 1020,
        53, 2, 1060, 12, 2020, 4020, 1030, 2040, 52, 3020, 8040, 1050, 2000, 2010, 5040, 3000, 5010, 6020, 2050,
        3050, 5042, 3040, 5002, 83, 5043, 5012, 4040, 5000, 3010, 5013, 103, 5022, 62, 6050, 5003, 1080, 4010,
        32, 1100, 5060, 113, 2060, 3060, 2030, 5052, 3030, 93, 5063, 1110, 72, 5062, 4000, 4060, 112, 73, 1090,
        6030, 82, 2070, 2110, 3110, 1070, 5080, 3070, 5032, 2080, 102, 5072, 3080, 6000, 5100, 92, 6110, 5082,
        6040, 2100, 5083, 4080, 5070, 5103, 5020, 2090, 4090, 5112, 6060, 5102, 5110, 4100, 5073, 5030, 5023,
        5050, 5090, 4070, 5113, 6080, 5033, 3100, 6010, 6090, 5053, 5093, 3090, 5092, 7020, 6100, 6070, 7090,
    ),
)


def moment_step(gradient, moment_one, moment_two):
    moment_one = 0.9 * moment_one + 0.1 * gradient
    moment_two = 0.95 * moment_two + 0.05 * gradient * gradient
    return moment_one, moment_two


def weight_step(moment_one, moment_two, weight):
    update = moment_one / (1.0 - 0.9**50) / (jnp.sqrt(moment_two / (1.0 - 0.95**50)) + 1e-08)
    return weight - 0.05 * (update + 0.1 * weight)


class Chunk(typing.NamedTuple):
    row: int
    col: int
    width: int
    early: bool
    split: bool
    ahead: bool


def job_list(dp, chunks, role):
    jobs = []
    for c, chunk in enumerate(chunks):
        jobs += [("U", c, k) for k in range(dp - 1, role, -1)] + [("D", c, k) for k in range(role)] + [("X", c, 0)]
        passed = [("F", c, k) for k in range(role - 1, -1, -1)]
        if role > 0:
            passed += [("F", c, k) for k in range(role + 1, dp)]
        if chunk.early:
            jobs += [("A", c, 0)] * chunk.ahead + [("M", c, 0)] + passed + [("W", c, 0), ("V", c, 0)]
        else:
            jobs += [("A", c, 0)] * chunk.ahead + [("W", c, 0)] * chunk.split + [("M", c, 0), ("V", c, 0)] + passed
            jobs += [("Z", c, 0)] * (chunk.split or role == 0)
    return jobs


def plan(dp, tile_rows, cols):
    tuned = (dp == len(ORDERS) * 2) and tile_rows == ROWS * len(PARTS) and cols % (128 * max(PARTS)) == 0
    parts = PARTS if tuned else (1,) * (tile_rows // ROWS)
    spans = [(i * ROWS, j * (cols // n), cols // n) for i, n in enumerate(parts) for j in range(n)]
    chunks = [
        Chunk(*span, *((EARLY[c] == 1, SPLIT[c] == 1, AHEAD[c] == 1) if tuned else (c % 2 == 0, False, False)))
        for c, span in enumerate(spans)
    ]
    orders = [job_list(dp, chunks, role) for role in range(dp // 2)]
    if tuned:
        orders = [
            [(KINDS[code // 1000], code // 10 % 100, code % 10) for code in coded] for coded in ORDERS
        ]
    start = [job[0] == "X" for job in orders[0]].index(True)
    orders[0][:start] = sorted(orders[0][:start], key=lambda job: job[0] != "U")
    return chunks, orders


def kernel(dp, peers, owners, chunks, orders, old_ref, new_ref, g_hbm, m_hbm, v_hbm, w_hbm, *rest):
    moments, params, rest = rest[0], rest[1], rest[2:]
    g, state, weights, part, line = rest[:5]
    rest = rest[5:]
    count = len(chunks)
    fresh, mail, inbox, wide, wide_mail, wide_inbox, old_mail, old_inbox = (
        rest[i * count : (i + 1) * count] for i in range(8)
    )
    g_sem, old_sem, in_sem, sent, z_recv, x_recv, w_recv, o_recv = rest[8 * count :]
    z = lax.axis_index("dp")
    e = lax.axis_index("expert")
    old_slots, cols = state.shape[1], state.shape[-1]
    new_slots = params.shape[0]
    far = jnp.where(z < dp // 2, 0, 1)
    place = jnp.where(z < dp // 2, z, dp - 1 - z)
    ahead = 1 - 2 * far
    owns = e < owners

    if peers & (peers - 1):
        targets = [lax.rem(e + step, peers) for step in range(peers)]
    else:
        bits = [1 << i for i in range(peers.bit_length() - 1)]
        turns = {bit: bit * (1 - 2 * lax.rem(e // bit, 2)) for bit in bits}
        targets = [e + sum(turns[bit] for bit in bits if mask & bit) for mask in (0, *range(peers - 1, 0, -1))]

    def rows(c):
        return pl.ds(chunks[c].row, ROWS)

    def span(c):
        return pl.ds(chunks[c].col, chunks[c].width)

    def real(k):
        return k + far * (dp - 1 - 2 * k)

    def block(c, k):
        return pl.ds(pl.multiple_of(real(k) * cols + chunks[c].col, 128), chunks[c].width)

    def wide_block(c, k, plane):
        return pl.ds(pl.multiple_of(lax.rem(k - plane + dp, dp) * chunks[c].width, 128), chunks[c].width)

    def mine(c):
        return pl.ds(pl.multiple_of(z * cols + chunks[c].col, 128), chunks[c].width)

    def way(right):
        return far if right else 1 - far

    def beside(right):
        return {"dp": z + ahead if right else z - ahead}

    g_loads = [
        pltpu.make_async_copy(g_hbm.at[0, :, pl.ds(row, ROWS)], g.at[:, pl.ds(row, ROWS)], g_sem.at[row // ROWS])
        for row in range(0, g.shape[1], ROWS)
    ]
    loads = [pltpu.make_async_copy(w_hbm, weights, old_sem)]
    loads += [pltpu.make_async_copy(ref, state.at[i], in_sem) for i, ref in enumerate((m_hbm, v_hbm))]

    @pl.when(owns)
    def _():
        g_loads[0].start()

    barrier = pltpu.get_barrier_semaphore()
    for to in targets[1:]:
        pl.semaphore_signal(barrier, inc=1, device_id={"expert": to}, device_id_type=MESH)
    for step in (-1, 1):
        @pl.when((z + step >= 0) & (z + step < dp))
        def _():
            pl.semaphore_signal(barrier, inc=1, device_id={"dp": z + step}, device_id_type=MESH)

    @pl.when(owns)
    def _():
        for load in g_loads[1:3] + loads[:1] + g_loads[3:] + loads[1:]:
            load.start()

    inner = (z > 0).astype(jnp.int32) + (z < dp - 1).astype(jnp.int32)
    pl.semaphore_wait(barrier, peers - 1 + inner)

    def route(tile, carry):
        sent, taken, slots, sources = carry
        old, new = old_ref[tile], new_ref[tile]
        leaves, comes = old == e, new == e
        slots = tuple(jnp.where(leaves & (new == to), sent, slot) for to, slot in zip(targets, slots))
        sources = tuple(
            jnp.where(comes & (taken == slot), old, source) for slot, source in enumerate(sources)
        )
        return sent + leaves.astype(jnp.int32), taken + comes.astype(jnp.int32), slots, sources

    def taken_by(sem, ref):
        pltpu.make_async_copy(ref, ref, sem).wait()

    def sum_copy(c, k, right, raw=False):
        src = g.at[:, rows(c), block(c, k)] if raw else part.at[real(k), :, rows(c), span(c)]
        return pltpu.make_async_remote_copy(
            src, line.at[way(right), real(k), :, rows(c), span(c)], sent, z_recv.at[c, real(k)],
            device_id=beside(right), device_id_type=MESH,
        )

    def gather_copy(c, k, right, to_end):
        src = dst = params.at[:, rows(c), block(c, k)]
        if chunks[c].early:
            src = wide[c].at[:, :, wide_block(c, real(k), z)]
            dst = wide[c].at[:, :, wide_block(c, real(k), beside(right)["dp"])]
        return pltpu.make_async_remote_copy(
            src, dst, sent, z_recv.at[c, real(1 if to_end else k)],
            device_id=beside(right), device_id_type=MESH,
        )

    def gather_send(c, k, right, role):
        gather_copy(c, k, right, role == 1 and not right).start()

    def gather_bytes(c, pieces):
        ref = g if chunks[c].early else params
        return ref.at[:, pl.ds(0, pieces * ROWS), pl.ds(0, chunks[c].width)]

    def mail_copy(c, to):
        return pltpu.make_async_remote_copy(
            mail[c].at[to], inbox[c].at[e], sent, x_recv.at[c],
            device_id={"expert": to}, device_id_type=MESH,
        )

    def mail_bytes(c, boxes):
        return mail[c].at[pl.ds(0, boxes)]

    def weights_copy(c, to):
        return pltpu.make_async_remote_copy(
            wide_mail[c].at[to], wide_inbox[c].at[e], sent, w_recv.at[c],
            device_id={"expert": to}, device_id_type=MESH,
        )

    def old_copy(c, to):
        return pltpu.make_async_remote_copy(
            old_mail[c].at[to], old_inbox[c].at[e], sent, o_recv.at[c],
            device_id={"expert": to}, device_id_type=MESH,
        )

    def weights_bytes(c, boxes):
        return wide_mail[c].at[pl.ds(0, boxes)]

    def arrived(c, k, right):
        return line[way(right), real(k), :, rows(c), span(c)].astype(jnp.float32)

    def add_and_send(c, k, right):
        sum_copy(c, k, right).wait_recv()
        total = g[:, rows(c), block(c, k)].astype(jnp.float32) + arrived(c, k, right)
        part[real(k), :, rows(c), span(c)] = total.astype(jnp.bfloat16)
        sum_copy(c, k, right).start()

    def gather(c, role):
        gather_send(c, role, True, role)
        if role > 0:
            gather_send(c, role, False, role)

    def update(c, role):
        sides = [right for right in (True, False) if role > 0 or not right]
        at = line.at[pl.ds(0, len(sides)), z, :, rows(c), span(c)]
        taken_by(z_recv.at[c, z], at)
        for slot in range(old_slots):
            gradient = g[slot, rows(c), mine(c)].astype(jnp.float32)
            for right in sides:
                gradient += line[way(right), z, slot, rows(c), span(c)].astype(jnp.float32)
            values = list(moment_step(gradient, *(state[i, slot, rows(c), span(c)] for i in range(2))))
            if chunks[c].early or not chunks[c].ahead:
                values.insert(0, weight_step(*values, weights[slot, rows(c), span(c)]))
            values = [value.astype(jnp.bfloat16) for value in values]
            if chunks[c].early:
                wide[c][slot, :, pl.ds(0, chunks[c].width)] = values.pop(0)
            elif chunks[c].split:
                wide[c][slot] = values.pop(0)
            for i, value in enumerate(values):
                fresh[c][slot, i] = value
        if chunks[c].early:
            gather(c, role)

    def post(c, slots):
        for to, slot in zip(targets[1:], slots[1:]):
            mail[c][to] = fresh[c][slot]
            mail_copy(c, to).start()
        inbox[c][e] = fresh[c][slots[0]]

    def last_arrivals(c, role):
        if role == 0:
            taken_by(z_recv.at[c, real(1)], gather_bytes(c, dp - 1))

    def post_old_weights(c, slots):
        for to, slot in zip(targets[1:], slots[1:]):
            old_mail[c][to] = weights[slot, rows(c), span(c)].astype(jnp.bfloat16)
            old_copy(c, to).start()
        old_inbox[c][e] = weights[slots[0], rows(c), span(c)].astype(jnp.bfloat16)

    def post_weights(c, role, slots):
        if chunks[c].early:
            last_arrivals(c, role)
        size = wide_mail[c].shape[2]
        columns = pl.ds(wide[c].shape[2] - size, size)
        for to, slot in zip(targets[1:], slots[1:]):
            wide_mail[c][to] = wide[c][slot, :, columns]
            weights_copy(c, to).start()
        wide_inbox[c][e] = wide[c][slots[0], :, columns]

    def receive(c, moments_too, weights_too, old_too):
        for mask, boxes in ((owns, owners - 1), (e >= owners, owners)):
            @pl.when(mask)
            def _():
                if moments_too:
                    taken_by(x_recv.at[c], mail_bytes(c, boxes))
                if weights_too:
                    taken_by(w_recv.at[c], weights_bytes(c, boxes))
                if old_too:
                    taken_by(o_recv.at[c], old_mail[c].at[pl.ds(0, boxes)])

    def kept(slot, taken, value):
        return jnp.where(taken > slot, value, jnp.zeros_like(value))

    def place_moments(c, taken, sources):
        first = inbox[c].shape[1] - 2
        for slot in range(new_slots):
            for i in range(2):
                moments[i, slot, rows(c), span(c)] = kept(slot, taken, inbox[c][sources[slot], first + i])

    def deliver(c, role, taken, sources):
        width = chunks[c].width
        receive(c, not chunks[c].split, chunks[c].early or chunks[c].split, chunks[c].ahead)
        for slot in range(new_slots):
            if chunks[c].ahead:
                values = [inbox[c][sources[slot], i] for i in range(2)] + [old_inbox[c][sources[slot]]]
                own = weight_step(*(value.astype(jnp.float32) for value in values)).astype(jnp.bfloat16)
            elif chunks[c].early:
                own = wide_inbox[c][sources[slot], :, pl.ds(0, width)]
            else:
                own = wide_inbox[c][sources[slot]] if chunks[c].split else inbox[c][sources[slot], 0]
            params[slot, rows(c), mine(c)] = kept(slot, taken, own)
            for step in range(1, dp if chunks[c].early else 1):
                column = pl.multiple_of(lax.rem(z + step, dp) * cols + chunks[c].col, 128)
                first = (step - 1 if chunks[c].ahead else step) * width
                value = wide_inbox[c][sources[slot], :, pl.ds(first, width)]
                params[slot, rows(c), pl.ds(column, width)] = kept(slot, taken, value)
        if not chunks[c].early:
            gather(c, role)
        if not chunks[c].split:
            place_moments(c, taken, sources)

    def finish(c, role, taken, sources):
        if chunks[c].split:
            receive(c, True, False, False)
            place_moments(c, taken, sources)
        last_arrivals(c, role)

    def run(role, order, slots, taken, sources, loaded):
        for kind, c, k in order:
            by_owners = kind in "UDXMWA" or (kind == "F" and chunks[c].early)

            def job():
                if kind in "UDX" and chunks[c].row not in loaded:
                    loaded.append(chunks[c].row)
                    g_loads[chunks[c].row // ROWS].wait()
                if kind in "XA" and -1 not in loaded:
                    loaded.append(-1)
                    loads[0].wait()
                if kind == "X" and -2 not in loaded:
                    loaded.append(-2)
                    taken_by(in_sem, state)
                if kind == "U" and role == 0:
                    sum_copy(c, k, True, True).start()
                elif kind in "UD":
                    add_and_send(c, k, kind == "U")
                elif kind == "X":
                    update(c, role)
                elif kind == "A":
                    post_old_weights(c, slots)
                elif kind == "M":
                    post(c, slots)
                elif kind == "F":
                    gather_copy(c, k, k < role, False).wait_recv()
                    gather_send(c, k, k < role, role)
                elif kind == "W":
                    post_weights(c, role, slots)
                elif kind == "V":
                    deliver(c, role, taken, sources)
                else:
                    finish(c, role, taken, sources)

            if by_owners:
                pl.when(owns)(job)
            else:
                job()

    lead = 0
    while orders[0][lead][0] == "U":
        lead += 1
    loaded = [[] for _ in orders]

    @pl.when(place == 0)
    def _():
        run(0, orders[0][:lead], None, None, None, loaded[0])

    zero = jnp.int32(0)
    _, taken, slots, sources = lax.fori_loop(
        0, old_ref.shape[0], route, (zero, zero, (zero,) * peers, (zero,) * new_slots)
    )
    slots = tuple(jnp.minimum(slot, old_slots - 1) for slot in slots)
    sources = tuple(jnp.minimum(source, owners - 1) for source in sources)

    for role, order in enumerate(orders):
        @pl.when(place == role)
        def _():
            run(role, order[lead:] if role == 0 else order, slots, taken, sources, loaded[role])

            def gathers_sent(c):
                taken_by(sent, gather_bytes(c, dp + 1 if role > 0 else 1))

            for c in range(count):
                if not chunks[c].early:
                    gathers_sent(c)

            @pl.when(owns)
            def _():
                for c in range(count):
                    if chunks[c].early:
                        gathers_sent(c)

    @pl.when(owns)
    def _():
        taken_by(sent, part.at[pl.ds(0, dp - 1)])
        for c in range(count):
            taken_by(sent, mail_bytes(c, peers - 1))
            if chunks[c].early or chunks[c].split:
                taken_by(sent, weights_bytes(c, peers - 1))
            if chunks[c].ahead:
                taken_by(sent, old_mail[c].at[pl.ds(0, peers - 1)])


def widen(moments, params, w_out, m_out, v_out, p_out, staged, sems):
    new_slots, _, cols = w_out.shape
    z = lax.axis_index("dp")
    mine = pl.ds(pl.multiple_of(z * cols, cols), cols)
    pltpu.make_async_copy(params, p_out, sems.at[3]).start()
    for slot in range(new_slots):
        parts = (params.at[slot, :, mine], moments.at[0, slot], moments.at[1, slot])
        for i, (part, out) in enumerate(zip(parts, (w_out, m_out, v_out))):
            staged[i, slot] = part[...].astype(jnp.float32)
            pltpu.make_async_copy(staged.at[i, slot], out.at[slot], sems.at[i]).start()
    for i, out in enumerate((w_out, m_out, v_out, p_out)):
        pltpu.make_async_copy(out, out, sems.at[i]).wait()


def shards(grad_parts, first_moment, second_moment, master_weight, old_owner, new_owner):
    dp = lax.axis_size("dp")
    peers = lax.axis_size("expert")
    old_slots, tile_rows, cols = first_moment.shape
    owners = old_owner.shape[0] // old_slots
    new_slots = min(old_slots + old_slots // 2, peers - peers // 5)
    chunks, orders = plan(dp, tile_rows, cols)
    count = len(chunks)
    bf16, f32 = jnp.bfloat16, jnp.float32
    dma = pltpu.SemaphoreType.DMA
    any_space = pl.BlockSpec(memory_space=pl.ANY)
    smem = pl.BlockSpec(memory_space=pltpu.SMEM)
    vmem = pl.BlockSpec(memory_space=pltpu.VMEM)
    master = jax.ShapeDtypeStruct((new_slots, tile_rows, cols), f32)
    scratch = [
        pltpu.VMEM((old_slots, tile_rows, dp * cols), bf16),
        pltpu.VMEM((2, old_slots, tile_rows, cols), f32),
        pltpu.VMEM((old_slots, tile_rows, cols), f32),
        pltpu.VMEM((dp, old_slots, tile_rows, cols), bf16),
        pltpu.VMEM((2, dp, old_slots, tile_rows, cols), bf16),
    ]
    kept = [2 if chunk.early or chunk.split or chunk.ahead else 3 for chunk in chunks]
    wide = [chunk.width * (dp if chunk.early else 1) if chunk.early or chunk.split else 128 for chunk in chunks]
    sent = [size - chunk.width if chunk.early and chunk.ahead else size for size, chunk in zip(wide, chunks)]
    old = [chunk.width if chunk.ahead else 128 for chunk in chunks]
    for boxes in (old_slots, peers, owners):
        scratch += [pltpu.VMEM((boxes, n, ROWS, chunk.width), bf16) for n, chunk in zip(kept, chunks)]
    for boxes, sizes in ((old_slots, wide), (peers, sent), (owners, sent), (peers, old), (owners, old)):
        scratch += [pltpu.VMEM((boxes, ROWS, n), bf16) for n in sizes]
    scratch += [dma((tile_rows // ROWS,)), dma, dma, dma, dma((count, dp))]
    scratch += [dma((count,))] * 3
    results = new_slots * tile_rows * cols * (4 + 2 * dp)
    moments, params = pl.pallas_call(
        functools.partial(kernel, dp, peers, owners, chunks, orders),
        out_shape=(
            pltpu.VMEM((2, new_slots, tile_rows, cols), bf16),
            pltpu.VMEM((new_slots, tile_rows, dp * cols), bf16),
        ),
        in_specs=[smem] * 2 + [any_space] * 4,
        out_specs=(vmem,) * 2,
        scratch_shapes=scratch,
        compiler_params=pltpu.CompilerParams(
            collective_id=0, has_side_effects=True, vmem_limit_bytes=67043328 - results - 2**19
        ),
    )(old_owner, new_owner, grad_parts, first_moment, second_moment, master_weight)
    return pl.pallas_call(
        widen,
        out_shape=(master,) * 3
        + (jax.ShapeDtypeStruct((new_slots, tile_rows, dp * cols), bf16),),
        in_specs=[vmem] * 2,
        out_specs=(any_space,) * 4,
        scratch_shapes=[pltpu.VMEM((3, new_slots, tile_rows, cols), f32), dma((4,))],
        compiler_params=pltpu.CompilerParams(vmem_limit_bytes=2**24),
    )(moments, params)


def solution(mesh):
    placed = (
        P("dp", "expert", None, None),
        P("expert", None, "dp"),
        P("expert", None, "dp"),
        P("expert", None, "dp"),
        P(),
        P(),
    )
    return jax.shard_map(
        shards,
        mesh=mesh,
        in_specs=placed,
        out_specs=(
            P("expert", None, "dp"),
            P("expert", None, "dp"),
            P("expert", None, "dp"),
            P("expert", None, None),
        ),
        check_vma=False,
    )
```
